32 devices in a mesh: blk: 8 (over z, y), pair: 4 (over x, core).
Axes of the slice: x: 2, y: 2, z: 4, core: 2. Of those that a mesh axis runs over, the one named last changes fastest.
Arguments:
- amplitudes: bfloat16 [64, 262144], P('pair', 'blk'), may hold values from -6 to 6
- integrals: bfloat16 [5120, 4, 128, 128], P(('blk', 'pair')), may hold values from -0.25 to 0.25
- block_irrep: int32 [2048], replicated, may hold values from 0 to 7
- slab_blocks: int32 [32], replicated, may hold values from 0 to 2047, as said below
- owner: int32 [2048], replicated, may hold values from 0 to 31, as said below
- partner: int32 [2048], replicated, may hold values from 0 to 2047, as said below
- sign: int32 [2048], replicated, may hold values from -1 to 1, as said below
Outputs:
- ladder: bfloat16 [64, 262144], P('pair', 'blk')
The draws below stay inside these ranges and needn't reach their ends.
Inputs may be any that keep to these rules, and one draw needn't show every extreme that they name: Distinct blocks; block_irrep[slab_blocks[g * 4 + k]] = g. `owner`: flat device index (blk index times the pair axis's size plus pair index). For each blk index t, of the blocks t * 256 to t * 256 + 255 exactly 256 divided by the pair axis's size are stored on each pair index, at most 20 on any one device, and some device stores exactly 20 of them for every t. Integral rows not named by any block are read by no output. An involution without fixed points; for any blk indices t and t2, equal or not, exactly 256 divided by the blk axis's size of the blocks of t have their partner among the blocks of t2. `sign`: each entry is -1 or 1.
All inputs are finite; a program needn't handle non-finite values.
Results may differ from the reference program's by a relative error of at most 0.001.
Values may be sent and summed in bfloat16 or wider, within the bound.
A program may use at most 128 MiB of HBM per device.

```python
import jax
import jax.numpy as jnp
from jax import lax

W = 128
IRREPS = 8
CPI = 4
BLK_DEV = 256
NB = 2048
PAIRS = 64
CAP = 20
SLOTS = 160
N_BLK = 8
N_PAIR = 4
DEVICES = 32


def irrep_layout(key):
    base = jax.random.fold_in(key, 7)
    shuffled = jax.random.permutation(jax.random.fold_in(base, 1), NB)
    others = jax.random.randint(jax.random.fold_in(base, 2), (NB,), 0, IRREPS)
    position_ids = jnp.arange(NB)
    label_at = jnp.where(position_ids < IRREPS * CPI, position_ids // CPI, others).astype(jnp.int32)
    labels = jnp.zeros((NB,), jnp.int32).at[shuffled].set(label_at)
    chosen = shuffled[:IRREPS * CPI].astype(jnp.int32)
    return (labels, chosen)


def draw_block_irrep(key, part):
    labels, chosen = irrep_layout(key)
    return labels


def draw_slab_blocks(key, part):
    labels, chosen = irrep_layout(key)
    return chosen


def draw_owner(key, part):
    base = jax.random.fold_in(key, 11)
    heavy_order = jax.random.permutation(jax.random.fold_in(base, 1), N_BLK)
    range_keys = jax.random.split(jax.random.fold_in(base, 2), N_BLK)
    shuffles = jax.vmap(lambda one_key: jax.random.permutation(one_key, BLK_DEV))(range_keys)
    local_ids = jnp.arange(BLK_DEV)
    group_len = BLK_DEV // N_PAIR
    stored_pair = local_ids // group_len
    within = local_ids % group_len
    light_count = BLK_DEV // (2 * DEVICES)
    heavy_total = 5 * light_count * (N_BLK // 4)
    place = jnp.where(within < heavy_total, within // (5 * light_count), N_BLK // 4 + (within - heavy_total) // light_count)
    stored_blk = heavy_order[place]
    flat_device = (stored_blk * N_PAIR + stored_pair).astype(jnp.int32)
    range_rows = jnp.broadcast_to(jnp.arange(N_BLK)[:, None], (N_BLK, BLK_DEV))
    grid = jnp.zeros((N_BLK, BLK_DEV), jnp.int32).at[range_rows, shuffles].set(jnp.broadcast_to(flat_device[None, :], (N_BLK, BLK_DEV)))
    return grid.reshape(NB)


def draw_partner(key, part):
    base = jax.random.fold_in(key, 13)
    range_keys = jax.random.split(base, N_BLK)
    shuffles = jax.vmap(lambda one_key: jax.random.permutation(one_key, BLK_DEV))(range_keys)
    group_len = BLK_DEV // N_BLK
    block_grid = (jnp.arange(N_BLK)[:, None] * BLK_DEV + shuffles).astype(jnp.int32).reshape(N_BLK, N_BLK, group_len)
    mates = jnp.swapaxes(block_grid, 0, 1)
    rolled = jnp.roll(block_grid, group_len // 2, axis=2)
    diagonal = (jnp.arange(N_BLK)[:, None] == jnp.arange(N_BLK)[None, :])[:, :, None]
    mates = jnp.where(diagonal, rolled, mates)
    return jnp.zeros((NB,), jnp.int32).at[block_grid.reshape(-1)].set(mates.reshape(-1))


def draw_sign(key, part):
    coins = jax.random.randint(jax.random.fold_in(key, 17), (NB,), 0, 2)
    return (2 * coins - 1).astype(jnp.int32)


def shard_levels(stream_key, shape, cuts, least, largest):
    loudness = 1.0
    for position, shards_of in cuts:
        draws = jax.random.uniform(jax.random.fold_in(jax.random.fold_in(stream_key, 6), position), (shards_of,), jnp.float32, least / len(cuts), largest / len(cuts))
        loudness = loudness * jnp.repeat(jnp.exp(draws), shape[position] // shards_of).reshape((-1,) + (1,) * (len(shape) - 1 - position))
    return loudness


def centred(key, extent, scale, limit, shards=(), held_as=jnp.bfloat16):
    factor_of = shard_levels(key, extent, shards, -0.22, 0.18) if shards else 1.0
    drawn = jax.random.normal(key, extent, jnp.float32) * scale * factor_of
    return jnp.minimum(jnp.maximum(drawn, -limit), limit).astype(held_as)


def setup_inputs(seed: int = 0) -> dict:
    keys = jax.random.split(jax.random.key(seed), 8)
    amplitudes = centred(keys[0], (PAIRS, NB * W), 1.0, 6.0, ((0, 4), (1, 8)))
    integrals = centred(keys[1], (DEVICES * SLOTS, CPI, W, W), (CPI * W) ** -0.5, 0.25, ((0, 32),))
    block_irrep = draw_block_irrep(jax.random.fold_in(keys[7], 71), 0)
    slab_blocks = draw_slab_blocks(jax.random.fold_in(keys[7], 71), 0)
    owner = draw_owner(jax.random.fold_in(keys[7], 71), 0)
    partner = draw_partner(jax.random.fold_in(keys[7], 71), 0)
    sign = draw_sign(jax.random.fold_in(keys[7], 71), 0)
    return {"amplitudes": amplitudes, "integrals": integrals, "block_irrep": block_irrep, "slab_blocks": slab_blocks, "owner": owner, "partner": partner, "sign": sign}


def earlier_matches(labels):
    span_length = labels.shape[1]
    position_ids = jnp.arange(span_length, dtype=jnp.int32)
    earlier_mask = position_ids[None, :] < position_ids[:, None]
    same_label = labels[:, :, None] == labels[:, None, :]
    return jnp.sum(jnp.logical_and(same_label, earlier_mask[None]), axis=2).astype(jnp.int32)


def reference(amplitudes, integrals, block_irrep, slab_blocks, owner, partner, sign):
    block_ids = jnp.arange(NB, dtype=jnp.int32)
    block_ranks = earlier_matches(owner.reshape(N_BLK, BLK_DEV)).reshape(NB)
    tile_rows = (owner * SLOTS + (block_ids // BLK_DEV) * CAP + block_ranks).astype(jnp.int32)
    amp_blocks = amplitudes.reshape(PAIRS, NB, W)
    slab_matrix = jnp.take(amp_blocks, slab_blocks, axis=1).reshape(PAIRS, IRREPS, CPI * W)
    batch_size = BLK_DEV // 4

    def one_batch(chosen):
        tile_batch = jnp.take(integrals, jnp.take(tile_rows, chosen), axis=0).reshape(batch_size, CPI * W, W)
        slab_batch = jnp.take(slab_matrix, jnp.take(block_irrep, chosen), axis=1)
        return jnp.einsum("pbk,bkw->bpw", slab_batch.astype(jnp.float32), tile_batch.astype(jnp.float32))

    products = lax.map(one_batch, block_ids.reshape(NB // batch_size, batch_size)).reshape(NB, PAIRS, W)
    facing = jnp.take(products, partner, axis=0)
    mirrored = jnp.roll(facing, PAIRS // 2, axis=1)
    summed = products + sign.astype(jnp.float32)[:, None, None] * mirrored
    return jnp.transpose(summed.astype(jnp.bfloat16), (1, 0, 2)).reshape(PAIRS, NB * W)
```

```python
import functools

import jax
import jax.numpy as jnp
from jax import lax
from jax.experimental import pallas as pl
from jax.experimental.pallas import tpu as pltpu
from jax.sharding import PartitionSpec as P

TOP = 32766.0
TINY = 2.0**-110
MESH = pl.DeviceIdType.MESH
HALVES = 2


def unroll_of(trips, most):
    return max(n for n in range(1, most + 1) if trips % n == 0)


def prep_kernel(
    sizes,
    slab_ref,
    owner_ref,
    partner_ref,
    irrep_ref,
    sign_ref,
    amp_hbm,
    irrep_out,
    meta_out,
    picked,
    raw,
    pick_sem,
):
    blks, pairs, span, cap, per_irrep, slab_count, rows, width = sizes
    me_blk = lax.axis_index("blk")
    me = me_blk * pairs + lax.axis_index("pair")

    def pick(n):
        at = jnp.clip(slab_ref[n] - me_blk * span, 0, span - 1) * width
        return pltpu.make_async_copy(
            amp_hbm.at[:, pl.ds(pl.multiple_of(at, width), width)], raw.at[n], pick_sem.at[n]
        )

    for n in range(slab_count):
        pick(n).start()

    down = lax.broadcasted_iota(jnp.int32, (span, span), 0)
    across = lax.broadcasted_iota(jnp.int32, (span, span), 1)
    diagonal = down == across
    earlier = down < across

    def column(row):
        return jnp.sum(jnp.where(diagonal, row, 0.0), axis=1, keepdims=True)

    def count(mask):
        return jnp.sum(jnp.where(mask, 1.0, 0.0), axis=0, keepdims=True)

    def placed(keys, values):
        hit = keys == across.astype(jnp.float32)
        return jnp.sum(jnp.where(hit, values, 0.0), axis=0, keepdims=True)

    parts = span // width

    def mine(ref):
        found = [ref[pl.ds(me_blk * parts + part, 1), :] for part in range(parts)]
        return jnp.concatenate(found, axis=1).astype(jnp.float32)

    def every(ref):
        found = [ref[pl.ds(part, blks, stride=parts), :] for part in range(parts)]
        return jnp.concatenate(found, axis=1)

    owner, partner, sign = mine(owner_ref), mine(partner_ref), mine(sign_ref)
    partner_blk = jnp.floor((partner + 0.5) * (1.0 / span))
    owner_col, partner_col, blk_col = column(owner), column(partner), column(partner_blk)
    same_blk = blk_col == partner_blk
    rank = count(jnp.logical_and(owner_col == owner, earlier))
    send_key = partner_blk * (span // blks) + count(jnp.logical_and(same_blk, earlier))
    mirror_rank = count(jnp.logical_and(same_blk, partner_col < partner))
    key_col = column(send_key)
    send_dev = placed(key_col, owner_col)
    send_rank = placed(key_col, column(rank))
    capw, glenw = -(-cap // 2), span // blks // 2
    table = []
    for index, count_of, place in (
        (owner, capw, rank),
        (send_dev, capw, send_rank),
        (partner_blk, glenw, mirror_rank),
    ):
        word = jnp.floor(place * 0.5)
        shift = 16.0 - 16.0 * (place - 2.0 * word)
        table += [index, place, index * count_of + word, shift]
    for at, row in enumerate(table + [sign]):
        meta_out[at : at + 1, :] = row.astype(jnp.int32)

    stored = every(owner_ref) == me
    ranks = jnp.dot(
        jnp.where(stored, 1.0, 0.0).astype(jnp.bfloat16),
        jnp.where(earlier, 1.0, 0.0).astype(jnp.bfloat16),
        preferred_element_type=jnp.float32,
    ).astype(jnp.int32)
    ranks = jnp.where(stored, ranks, -1)
    irrep = every(irrep_ref).astype(jnp.float32)
    lane = lax.broadcasted_iota(jnp.int32, (blks, width), 1)
    slots = jnp.zeros((blks, width), jnp.float32)
    for r in range(cap):
        found = jnp.sum(jnp.where(ranks == r, irrep, 0.0), axis=1, keepdims=True)
        slots = jnp.where(lane == r, found, slots)
    irrep_out[...] = slots.astype(jnp.int32)

    for n in range(slab_count):
        pick(n).wait()
    for n in range(slab_count):
        local = slab_ref[n] - me_blk * span
        inside = jnp.logical_and(local >= 0, local < span).astype(jnp.float32)
        picked[n] = (raw[n].astype(jnp.float32) * inside).astype(jnp.bfloat16)


def kernel(
    sizes,
    irrep_ref,
    meta_ref,
    picked,
    ints_hbm,
    out_ref,
    ints,
    picked_in,
    slab_in,
    slab,
    send1a,
    send1b,
    recv1a,
    recv1b,
    scale1,
    scale1_in,
    scale1_s,
    own,
    send2a,
    send2b,
    recv2a,
    recv2b,
    scale2_s,
    scale2,
    scale2_in,
    scale2_in_s,
    ints_sem,
    pick_send,
    pick_recv,
    gath_send,
    gath_recv,
    fwd_send,
    fwd_recv,
    send1_sem,
    recv1_sem,
    send2_sem,
    recv2_sem,
    table_sem,
):
    blks, pairs, span, cap, per_irrep, slab_count, rows, width = sizes
    devices = blks * pairs
    chunk = slab_count // blks
    glen = span // blks
    me_blk = lax.axis_index("blk")
    me_pair = lax.axis_index("pair")
    me = me_blk * pairs + me_pair
    capw, glenw, half = -(-cap // 2), glen // 2, rows // 2
    lane = lax.broadcasted_iota(jnp.int32, (1, width), 1)
    send1, recv1 = (send1a, send1b), (recv1a, recv1b)
    send2, recv2 = (send2a, send2b), (recv2a, recv2b)

    def blk_at(step):
        pattern = blks // 2 + (1 - step % 2) * (step // 2) - (step % 2) * ((step + 1) // 2)
        found, bit = 0, 1
        while bit < blks:
            found = found + lax.rem(me_blk // bit + pattern // bit, 2) * bit
            bit *= 2
        return found

    def ints_copy(step):
        at = blk_at(step)
        return pltpu.make_async_copy(
            ints_hbm.at[pl.ds(at * cap, cap)], ints.at[pl.ds(at * cap, cap)], ints_sem.at[step]
        )

    @pl.loop(0, blks)
    def _(step):
        ints_copy(step).start()

    barrier = pltpu.get_barrier_semaphore()

    @pl.loop(1, devices)
    def _(step):
        other = lax.rem(me + step, devices)
        pl.semaphore_signal(
            barrier,
            inc=1,
            device_id={"blk": other // pairs, "pair": lax.rem(other, pairs)},
            device_id_type=MESH,
        )

    pl.semaphore_wait(barrier, devices - 1)

    def pick_copy(step):
        to = blk_at(step)
        return pltpu.make_async_remote_copy(
            src_ref=picked.at[pl.ds(to * chunk, chunk)],
            dst_ref=picked_in.at[me_blk],
            send_sem=pick_send.at[step],
            recv_sem=pick_recv.at[step],
            device_id={"blk": to},
            device_id_type=MESH,
        )

    @pl.loop(0, blks - 1)
    def _(step):
        pick_copy(step).start()

    @pl.loop(0, blks - 1)
    def _(step):
        pick_copy(step).wait()

    total = picked[pl.ds(me_blk * chunk, chunk)].astype(jnp.float32)
    for step in range(blks - 1):
        total = total + picked_in[blk_at(step)].astype(jnp.float32)
    slab_in[me_pair, me_blk] = total.astype(jnp.bfloat16)

    def gath_copy(step):
        return pltpu.make_async_remote_copy(
            src_ref=slab_in.at[me_pair, me_blk],
            dst_ref=slab_in.at[me_pair, me_blk],
            send_sem=gath_send.at[step],
            recv_sem=gath_recv.at[step],
            device_id={"blk": blk_at(step)},
            device_id_type=MESH,
        )

    def fwd_copy(source_blk, step, turn):
        return pltpu.make_async_remote_copy(
            src_ref=slab_in.at[me_pair, source_blk],
            dst_ref=slab_in.at[me_pair, source_blk],
            send_sem=fwd_send.at[step, turn],
            recv_sem=fwd_recv.at[step, turn],
            device_id={"pair": lax.rem(me_pair + 1 + turn, pairs)},
            device_id_type=MESH,
        )

    @pl.loop(0, blks - 1)
    def _(step):
        gath_copy(step).start()

    for turn in range(pairs - 1):
        fwd_copy(me_blk, blks - 1, turn).start()


    @pl.loop(0, blks - 1)
    def _(step):
        gath_copy(step).wait_recv()
        for turn in range(pairs - 1):
            fwd_copy(blk_at(step), step, turn).start()

    @pl.loop(0, blks - 1)
    def _(step):
        gath_copy(step).wait_send()

    @pl.loop(0, blks)
    def _(step):
        for turn in range(pairs - 1):
            fwd_copy(blk_at(step), step, turn).wait()

    for n in range(slab_count):
        for p in range(pairs):
            slab[
                n // per_irrep,
                p * rows : (p + 1) * rows,
                (n % per_irrep) * width : (n % per_irrep + 1) * width,
            ] = slab_in[p, n // chunk, n % chunk]

    def products(to):
        def slots(j, scales):
            coded = []
            for turn in range(2):
                r = jnp.minimum(2 * j + turn, cap - 1)
                product = jnp.dot(
                    slab[irrep_ref[to, r]], ints[to * cap + r], preferred_element_type=jnp.float32
                )
                tiles, found = [], []
                for p in range(pairs):
                    tile = product[p * rows : (p + 1) * rows]
                    largest = jnp.max(jnp.abs(tile), axis=0, keepdims=True)
                    largest = jnp.maximum(jnp.max(largest, axis=1, keepdims=True), TINY)
                    tiles.append(jnp.round(tile * (TOP / largest)).astype(jnp.int32))
                    found.append(jnp.where(lane == r, largest * (1.0 / TOP), scales[p]))
                scales = tuple(found)
                coded.append(tiles)
            for p in range(pairs):
                word = (coded[0][p] & 0xFFFF) | (coded[1][p] << 16)
                for h in range(HALVES):
                    send1[h][(to * pairs + p) * capw + j] = word[h * half : (h + 1) * half]
            return scales

        start = tuple(jnp.zeros((1, width), jnp.float32) for _ in range(pairs))
        scales = lax.fori_loop(0, capw, slots, start, unroll=unroll_of(capw, 5))
        for p in range(pairs):
            scale1[to * pairs + p] = scales[p]

    def product_copy(h, step, turn):
        to = blk_at(step)
        to_pair = lax.rem(me_pair + turn, pairs)
        at = to * pairs + to_pair
        if h == HALVES:
            source, target = scale1.at[at], scale1_in.at[me]
        else:
            source = send1[h].at[pl.ds(at * capw, capw)]
            target = recv1[h].at[pl.ds(me * capw, capw)]
        return pltpu.make_async_remote_copy(
            src_ref=source,
            dst_ref=target,
            send_sem=send1_sem.at[h, step, turn],
            recv_sem=recv1_sem.at[h, step, turn],
            device_id={"blk": to, "pair": to_pair},
            device_id_type=MESH,
        )

    def keep_copy(h):
        if h == HALVES:
            source, target = scale1.at[me], scale1_in.at[me]
        else:
            source = send1[h].at[pl.ds(me * capw, capw)]
            target = recv1[h].at[pl.ds(me * capw, capw)]
        return pltpu.make_async_copy(source, target, send1_sem.at[h, blks - 1, 0])

    def send_products(h):
        @pl.loop(0, blks - 1)
        def _(step):
            for turn in range(pairs):
                product_copy(h, step, turn).start()

        keep_copy(h).start()
        for turn in range(1, pairs):
            product_copy(h, blks - 1, turn).start()

    def wait_products(h):
        keep_copy(h).wait()

        @pl.loop(0, blks - 1)
        def _(step):
            for turn in range(pairs):
                product_copy(h, step, turn).wait()

        for turn in range(1, pairs):
            product_copy(h, blks - 1, turn).wait()

    @pl.loop(0, blks - 1)
    def _(step):
        ints_copy(step).wait()
        products(blk_at(step))
        for h in (HALVES, 0):
            for turn in range(pairs):
                product_copy(h, step, turn).start()

    ints_copy(blks - 1).wait()
    products(me_blk)
    for h in (HALVES, 0):
        keep_copy(h).start()
        for turn in range(1, pairs):
            product_copy(h, blks - 1, turn).start()
    send_products(1)

    def mirror_copy(h, step):
        to = blk_at(step)
        if h == HALVES:
            source, target = scale2.at[to], scale2_in.at[me_blk]
        else:
            source = send2[h].at[pl.ds(to * glenw, glenw)]
            target = recv2[h].at[pl.ds(me_blk * glenw, glenw)]
        return pltpu.make_async_remote_copy(
            src_ref=source,
            dst_ref=target,
            send_sem=send2_sem.at[h, step],
            recv_sem=recv2_sem.at[h, step],
            device_id={"blk": to, "pair": lax.rem(me_pair + pairs // 2, pairs)},
            device_id_type=MESH,
        )

    def table_copy(source, target, at):
        return pltpu.make_async_copy(source, target, table_sem.at[at])

    def value_of(word, shift):
        return ((word << shift) >> 16).astype(jnp.float32)

    def gather(h):
        @pl.loop(0, blks)
        def _(step):
            to = blk_at(step)

            def entry(m, carry):
                i = to * glen + 2 * m
                low = recv1[h][meta_ref[6, i]] << meta_ref[7, i]
                high = recv1[h][meta_ref[6, i + 1]] << meta_ref[7, i + 1]
                send2[h][to * glenw + m] = lax.shift_right_logical(low, 16) | (high & -65536)
                return carry

            lax.fori_loop(0, glenw, entry, 0, unroll=unroll_of(glenw, 8))
            mirror_copy(h, step).start()

        def own_entry(i, carry):
            scale = scale1_s[meta_ref[0, i], 0, meta_ref[1, i]]
            own[h, i] = value_of(recv1[h][meta_ref[2, i]], meta_ref[3, i]) * scale
            return carry

        lax.fori_loop(0, span, own_entry, 0, unroll=unroll_of(span, 8))

    def finish(h):
        def out_entry(i, carry):
            scale = scale2_in_s[meta_ref[8, i], 0, meta_ref[9, i]] * meta_ref[12, i].astype(jnp.float32)
            mirrored = value_of(recv2[h][meta_ref[10, i]], meta_ref[11, i])
            total = own[h, i] + mirrored * scale
            columns = pl.ds(pl.multiple_of(i * width, width), width)
            out_ref[h * half : (h + 1) * half, columns] = total.astype(jnp.bfloat16)
            return carry

        lax.fori_loop(0, span, out_entry, 0, unroll=unroll_of(span, 8))

    wait_products(HALVES)
    table_copy(scale1_in, scale1_s, 0).start()
    table_copy(scale1_in, scale1_s, 0).wait()

    def scale_entry(i, carry):
        scale2_s[i // glen, 0, i % glen] = scale1_s[meta_ref[4, i], 0, meta_ref[5, i]]
        return carry

    lax.fori_loop(0, span, scale_entry, 0, unroll=unroll_of(span, 8))
    table_copy(scale2_s, scale2, 1).start()
    table_copy(scale2_s, scale2, 1).wait()

    @pl.loop(0, blks)
    def _(step):
        mirror_copy(HALVES, step).start()

    wait_products(0)
    gather(0)

    @pl.loop(0, blks)
    def _(step):
        mirror_copy(HALVES, step).wait()

    table_copy(scale2_in, scale2_in_s, 2).start()
    table_copy(scale2_in, scale2_in_s, 2).wait()
    wait_products(1)
    gather(1)
    for h in range(HALVES):

        @pl.loop(0, blks)
        def _(step):
            mirror_copy(h, step).wait()

        finish(h)


def local(amplitudes, integrals, block_irrep, slab_blocks, owner, partner, sign):
    rows, columns = amplitudes.shape
    slots, per_irrep, _, width = integrals.shape
    blks = lax.axis_size("blk")
    pairs = lax.axis_size("pair")
    devices = blks * pairs
    span = columns // width
    cap = slots // blks
    glen = span // blks
    slab_count = slab_blocks.shape[0]
    irreps = slab_count // per_irrep
    chunk = slab_count // blks
    inner = per_irrep * width
    capw, half = -(-cap // 2), rows // 2
    tables = [table.reshape(-1, width) for table in (owner, partner, block_irrep, sign)]

    sizes = (blks, pairs, span, cap, per_irrep, slab_count, rows, width)
    smem = pl.BlockSpec(memory_space=pltpu.SMEM)
    vmem = pl.BlockSpec(memory_space=pltpu.VMEM)
    dma = pltpu.SemaphoreType.DMA
    hbm = pl.BlockSpec(memory_space=pl.ANY)
    slot_irrep, meta, picked = pl.pallas_call(
        functools.partial(prep_kernel, sizes),
        out_shape=(
            jax.ShapeDtypeStruct((blks, width), jnp.int32),
            jax.ShapeDtypeStruct((16, span), jnp.int32),
            jax.ShapeDtypeStruct((slab_count, rows, width), jnp.bfloat16),
        ),
        in_specs=[smem] + [vmem] * 4 + [hbm],
        out_specs=(vmem, vmem, vmem),
        scratch_shapes=[
            pltpu.VMEM((slab_count, rows, width), jnp.bfloat16),
            dma((slab_count,)),
        ],
    )(slab_blocks, *tables, amplitudes)
    return pl.pallas_call(
        functools.partial(kernel, sizes),
        out_shape=jax.ShapeDtypeStruct((rows, columns), jnp.bfloat16),
        in_specs=[smem, smem, vmem, hbm],
        out_specs=vmem,
        scratch_shapes=[
            pltpu.VMEM((slots, inner, width), jnp.bfloat16),
            pltpu.VMEM((blks, chunk, rows, width), jnp.bfloat16),
            pltpu.VMEM((pairs, blks, chunk, rows, width), jnp.bfloat16),
            pltpu.VMEM((irreps, rows * pairs, inner), jnp.bfloat16),
            *[pltpu.VMEM((devices * capw, half, width), jnp.int32)] * 4,
            pltpu.VMEM((devices, 1, width), jnp.float32),
            pltpu.VMEM((devices, 1, width), jnp.float32),
            pltpu.SMEM((devices, 1, width), jnp.float32),
            pltpu.VMEM((HALVES, span, half, width), jnp.float32),
            *[pltpu.VMEM((span // 2, half, width), jnp.int32)] * 4,
            pltpu.SMEM((blks, 1, width), jnp.float32),
            pltpu.VMEM((blks, 1, width), jnp.float32),
            pltpu.VMEM((blks, 1, width), jnp.float32),
            pltpu.SMEM((blks, 1, width), jnp.float32),
            dma((blks,)),
            dma((blks,)),
            dma((blks,)),
            dma((blks,)),
            dma((blks,)),
            dma((blks, pairs)),
            dma((blks, pairs)),
            dma((HALVES + 1, blks, pairs)),
            dma((HALVES + 1, blks, pairs)),
            dma((HALVES + 1, blks)),
            dma((HALVES + 1, blks)),
            dma((3,)),
        ],
        compiler_params=pltpu.CompilerParams(
            collective_id=0, has_side_effects=True, vmem_limit_bytes=56 * 2**20
        ),
    )(
        slot_irrep,
        meta,
        picked,
        integrals.reshape(slots, inner, width),
    )


def solution(mesh):
    placed = (P("pair", "blk"), P(("blk", "pair"), None, None, None), P(), P(), P(), P(), P())
    return jax.shard_map(
        local, mesh=mesh, in_specs=placed, out_specs=P("pair", "blk"), check_vma=False
    )
```

```python
import functools

import jax
import jax.numpy as jnp
from jax import lax
from jax.experimental import pallas as pl
from jax.experimental.pallas import tpu as pltpu
from jax.sharding import PartitionSpec as P

TOP = 32766.0
TINY = 2.0**-110
MESH = pl.DeviceIdType.MESH
HALVES = 2


def unroll_of(trips, most):
    return max(n for n in range(1, most + 1) if trips % n == 0)


def fill_tables(sizes, owner_ref, partner_ref, irrep_ref, sign_ref, irrep_out, meta_out):
    blks, pairs, span, cap, per_irrep, slab_count, rows, width = sizes
    me_blk = lax.axis_index("blk")
    me = me_blk * pairs + lax.axis_index("pair")

    down = lax.broadcasted_iota(jnp.int32, (span, span), 0)
    across = lax.broadcasted_iota(jnp.int32, (span, span), 1)
    diagonal = down == across
    earlier = down < across

    def column(row):
        return jnp.sum(jnp.where(diagonal, row, 0.0), axis=1, keepdims=True)

    def count(mask):
        return jnp.sum(jnp.where(mask, 1.0, 0.0), axis=0, keepdims=True)

    def placed(keys, values):
        hit = keys == across.astype(jnp.float32)
        return jnp.sum(jnp.where(hit, values, 0.0), axis=0, keepdims=True)

    parts = span // width

    def mine(ref):
        found = [ref[pl.ds(me_blk * parts + part, 1), :] for part in range(parts)]
        return jnp.concatenate(found, axis=1).astype(jnp.float32)

    def every(ref):
        found = [
            jnp.concatenate([ref[b * parts + part : b * parts + part + 1, :] for b in range(blks)])
            for part in range(parts)
        ]
        return jnp.concatenate(found, axis=1)

    owner, partner, sign = mine(owner_ref), mine(partner_ref), mine(sign_ref)
    partner_blk = jnp.floor((partner + 0.5) * (1.0 / span))
    owner_col, partner_col, blk_col = column(owner), column(partner), column(partner_blk)
    same_blk = blk_col == partner_blk
    rank = count(jnp.logical_and(owner_col == owner, earlier))
    send_key = partner_blk * (span // blks) + count(jnp.logical_and(same_blk, earlier))
    mirror_rank = count(jnp.logical_and(same_blk, partner_col < partner))
    key_col = column(send_key)
    send_dev = placed(key_col, owner_col)
    send_rank = placed(key_col, column(rank))
    capw, glenw = -(-cap // 2), span // blks // 2
    table = []
    for index, most, count_of, place in (
        (owner, blks * pairs, capw, rank),
        (send_dev, blks * pairs, capw, send_rank),
        (partner_blk, blks, glenw, mirror_rank),
    ):
        index = jnp.clip(index, 0.0, most - 1.0)
        place = jnp.clip(place, 0.0, min(2 * count_of, width) - 1.0)
        word = jnp.floor(place * 0.5)
        shift = 16.0 - 16.0 * (place - 2.0 * word)
        table += [index, place, index * count_of + word, shift]
    for at, row in enumerate(table + [sign]):
        meta_out[at : at + 1, :] = row.astype(jnp.int32)

    stored = every(owner_ref) == me
    ranks = jnp.dot(
        jnp.where(stored, 1.0, 0.0).astype(jnp.bfloat16),
        jnp.where(earlier, 1.0, 0.0).astype(jnp.bfloat16),
        preferred_element_type=jnp.float32,
    ).astype(jnp.int32)
    ranks = jnp.where(stored, ranks, -1)
    irrep = every(irrep_ref).astype(jnp.float32)
    lane = lax.broadcasted_iota(jnp.int32, (blks, width), 1)
    slots = jnp.zeros((blks, width), jnp.float32)
    for r in range(cap):
        found = jnp.sum(jnp.where(ranks == r, irrep, 0.0), axis=1, keepdims=True)
        slots = jnp.where(lane == r, found, slots)
    irrep_out[...] = slots.astype(jnp.int32)


def kernel(
    sizes,
    slab_ref,
    owner_ref,
    partner_ref,
    irreps_ref,
    sign_ref,
    amp_hbm,
    ints_hbm,
    out_ref,
    amp,
    amp_blocks,
    picked,
    irrep_v,
    meta_v,
    irrep_ref,
    meta_ref,
    ints,
    picked_in,
    slab_in,
    slab,
    send1a,
    send1b,
    recv1a,
    recv1b,
    scale1,
    scale1_in,
    scale1_s,
    own,
    send2a,
    send2b,
    recv2a,
    recv2b,
    scale2_s,
    scale2,
    scale2_in,
    scale2_in_s,
    ints_sem,
    pick_send,
    pick_recv,
    gath_send,
    gath_recv,
    fwd_send,
    fwd_recv,
    send1_sem,
    recv1_sem,
    send2_sem,
    recv2_sem,
    table_sem,
):
    blks, pairs, span, cap, per_irrep, slab_count, rows, width = sizes
    devices = blks * pairs
    chunk = slab_count // blks
    glen = span // blks
    me_blk = lax.axis_index("blk")
    me_pair = lax.axis_index("pair")
    me = me_blk * pairs + me_pair
    capw, glenw, half = -(-cap // 2), glen // 2, rows // 2
    lane = lax.broadcasted_iota(jnp.int32, (1, width), 1)
    send1, recv1 = (send1a, send1b), (recv1a, recv1b)
    send2, recv2 = (send2a, send2b), (recv2a, recv2b)

    def blk_at(step):
        pattern = blks // 2 + (1 - step % 2) * (step // 2) - (step % 2) * ((step + 1) // 2)
        found, bit = 0, 1
        while bit < blks:
            found = found + lax.rem(me_blk // bit + pattern // bit, 2) * bit
            bit *= 2
        return found

    def ints_copy(step):
        at = blk_at(step)
        return pltpu.make_async_copy(
            ints_hbm.at[pl.ds(at * cap, cap)], ints.at[pl.ds(at * cap, cap)], ints_sem.at[step]
        )

    def table_copy(source, target, at):
        return pltpu.make_async_copy(source, target, table_sem.at[at])

    table_copy(amp_hbm, amp, 0).start()

    @pl.loop(0, blks)
    def _(step):
        ints_copy(step).start()

    barrier = pltpu.get_barrier_semaphore()

    @pl.loop(1, devices)
    def _(step):
        other = lax.rem(me + step, devices)
        pl.semaphore_signal(
            barrier,
            inc=1,
            device_id={"blk": other // pairs, "pair": lax.rem(other, pairs)},
            device_id_type=MESH,
        )

    table_copy(amp_hbm, amp, 0).wait()

    def split(i, carry):
        amp_blocks[i] = amp[:, pl.ds(pl.multiple_of(i * width, width), width)]
        return carry

    lax.fori_loop(0, span, split, 0, unroll=unroll_of(span, 8))
    for n in range(slab_count):
        local = slab_ref[n] - me_blk * span
        inside = jnp.logical_and(local >= 0, local < span).astype(jnp.float32)
        block = amp_blocks[jnp.clip(local, 0, span - 1)]
        picked[n] = (block.astype(jnp.float32) * inside).astype(jnp.bfloat16)

    pl.semaphore_wait(barrier, devices - 1)

    def pick_copy(step):
        to = blk_at(step)
        return pltpu.make_async_remote_copy(
            src_ref=picked.at[pl.ds(to * chunk, chunk)],
            dst_ref=picked_in.at[me_blk],
            send_sem=pick_send.at[step],
            recv_sem=pick_recv.at[step],
            device_id={"blk": to},
            device_id_type=MESH,
        )

    @pl.loop(0, blks - 1)
    def _(step):
        pick_copy(step).start()

    fill_tables(sizes, owner_ref, partner_ref, irreps_ref, sign_ref, irrep_v, meta_v)
    table_copy(irrep_v, irrep_ref, 1).start()
    table_copy(meta_v, meta_ref, 2).start()

    @pl.loop(0, blks - 1)
    def _(step):
        pick_copy(step).wait()

    total = picked[pl.ds(me_blk * chunk, chunk)].astype(jnp.float32)
    for step in range(blks - 1):
        total = total + picked_in[blk_at(step)].astype(jnp.float32)
    slab_in[me_pair, me_blk] = total.astype(jnp.bfloat16)

    def gath_copy(step):
        return pltpu.make_async_remote_copy(
            src_ref=slab_in.at[me_pair, me_blk],
            dst_ref=slab_in.at[me_pair, me_blk],
            send_sem=gath_send.at[step],
            recv_sem=gath_recv.at[step],
            device_id={"blk": blk_at(step)},
            device_id_type=MESH,
        )

    def fwd_copy(source_blk, step, turn):
        return pltpu.make_async_remote_copy(
            src_ref=slab_in.at[me_pair, source_blk],
            dst_ref=slab_in.at[me_pair, source_blk],
            send_sem=fwd_send.at[step, turn],
            recv_sem=fwd_recv.at[step, turn],
            device_id={"pair": lax.rem(me_pair + 1 + turn, pairs)},
            device_id_type=MESH,
        )

    @pl.loop(0, blks - 1)
    def _(step):
        gath_copy(step).start()

    for turn in range(pairs - 1):
        fwd_copy(me_blk, blks - 1, turn).start()


    @pl.loop(0, blks - 1)
    def _(step):
        gath_copy(step).wait_recv()
        for turn in range(pairs - 1):
            fwd_copy(blk_at(step), step, turn).start()

    @pl.loop(0, blks - 1)
    def _(step):
        gath_copy(step).wait_send()

    @pl.loop(0, blks)
    def _(step):
        for turn in range(pairs - 1):
            fwd_copy(blk_at(step), step, turn).wait()

    for n in range(slab_count):
        for p in range(pairs):
            slab[
                n // per_irrep,
                p * rows : (p + 1) * rows,
                (n % per_irrep) * width : (n % per_irrep + 1) * width,
            ] = slab_in[p, n // chunk, n % chunk]

    table_copy(irrep_v, irrep_ref, 1).wait()
    table_copy(meta_v, meta_ref, 2).wait()

    def products(to):
        def slots(j, scales):
            coded = []
            for turn in range(2):
                r = jnp.minimum(2 * j + turn, cap - 1)
                product = jnp.dot(
                    slab[jnp.clip(irrep_ref[to, r], 0, slab_count // per_irrep - 1)], ints[to * cap + r], preferred_element_type=jnp.float32
                )
                tiles, found = [], []
                for p in range(pairs):
                    tile = product[p * rows : (p + 1) * rows]
                    largest = jnp.max(jnp.abs(tile), axis=0, keepdims=True)
                    largest = jnp.maximum(jnp.max(largest, axis=1, keepdims=True), TINY)
                    tiles.append(jnp.round(tile * (TOP / largest)).astype(jnp.int32))
                    found.append(jnp.where(lane == r, largest * (1.0 / TOP), scales[p]))
                scales = tuple(found)
                coded.append(tiles)
            for p in range(pairs):
                word = (coded[0][p] & 0xFFFF) | (coded[1][p] << 16)
                for h in range(HALVES):
                    send1[h][(to * pairs + p) * capw + j] = word[h * half : (h + 1) * half]
            return scales

        start = tuple(jnp.zeros((1, width), jnp.float32) for _ in range(pairs))
        scales = lax.fori_loop(0, capw, slots, start, unroll=unroll_of(capw, 5))
        for p in range(pairs):
            scale1[to * pairs + p] = scales[p]

    def product_copy(h, step, turn):
        to = blk_at(step)
        to_pair = lax.rem(me_pair + turn, pairs)
        at = to * pairs + to_pair
        if h == HALVES:
            source, target = scale1.at[at], scale1_in.at[me]
        else:
            source = send1[h].at[pl.ds(at * capw, capw)]
            target = recv1[h].at[pl.ds(me * capw, capw)]
        return pltpu.make_async_remote_copy(
            src_ref=source,
            dst_ref=target,
            send_sem=send1_sem.at[h, step, turn],
            recv_sem=recv1_sem.at[h, step, turn],
            device_id={"blk": to, "pair": to_pair},
            device_id_type=MESH,
        )

    def keep_copy(h):
        if h == HALVES:
            source, target = scale1.at[me], scale1_in.at[me]
        else:
            source = send1[h].at[pl.ds(me * capw, capw)]
            target = recv1[h].at[pl.ds(me * capw, capw)]
        return pltpu.make_async_copy(source, target, send1_sem.at[h, blks - 1, 0])

    def send_products(h):
        @pl.loop(0, blks - 1)
        def _(step):
            for turn in range(pairs):
                product_copy(h, step, turn).start()

        keep_copy(h).start()
        for turn in range(1, pairs):
            product_copy(h, blks - 1, turn).start()

    def wait_products(h):
        keep_copy(h).wait()

        @pl.loop(0, blks - 1)
        def _(step):
            for turn in range(pairs):
                product_copy(h, step, turn).wait()

        for turn in range(1, pairs):
            product_copy(h, blks - 1, turn).wait()

    @pl.loop(0, blks - 1)
    def _(step):
        ints_copy(step).wait()
        products(blk_at(step))
        for h in (HALVES, 0):
            for turn in range(pairs):
                product_copy(h, step, turn).start()

    ints_copy(blks - 1).wait()
    products(me_blk)
    for h in (HALVES, 0):
        keep_copy(h).start()
        for turn in range(1, pairs):
            product_copy(h, blks - 1, turn).start()
    send_products(1)

    def mirror_copy(h, step):
        to = blk_at(step)
        if h == HALVES:
            source, target = scale2.at[to], scale2_in.at[me_blk]
        else:
            source = send2[h].at[pl.ds(to * glenw, glenw)]
            target = recv2[h].at[pl.ds(me_blk * glenw, glenw)]
        return pltpu.make_async_remote_copy(
            src_ref=source,
            dst_ref=target,
            send_sem=send2_sem.at[h, step],
            recv_sem=recv2_sem.at[h, step],
            device_id={"blk": to, "pair": lax.rem(me_pair + pairs // 2, pairs)},
            device_id_type=MESH,
        )

    def value_of(word, shift):
        return ((word << shift) >> 16).astype(jnp.float32)

    def gather(h):
        @pl.loop(0, blks)
        def _(step):
            to = blk_at(step)

            def entry(m, carry):
                i = to * glen + 2 * m
                low = recv1[h][jnp.clip(meta_ref[6, i], 0, devices * capw - 1)] << meta_ref[7, i]
                high = recv1[h][jnp.clip(meta_ref[6, i + 1], 0, devices * capw - 1)] << meta_ref[7, i + 1]
                send2[h][to * glenw + m] = lax.shift_right_logical(low, 16) | (high & -65536)
                return carry

            lax.fori_loop(0, glenw, entry, 0, unroll=unroll_of(glenw, 8))
            mirror_copy(h, step).start()

        def own_entry(i, carry):
            scale = scale1_s[jnp.clip(meta_ref[0, i], 0, devices - 1), 0, jnp.clip(meta_ref[1, i], 0, width - 1)]
            own[h, i] = value_of(recv1[h][jnp.clip(meta_ref[2, i], 0, devices * capw - 1)], meta_ref[3, i]) * scale
            return carry

        lax.fori_loop(0, span, own_entry, 0, unroll=unroll_of(span, 8))

    def finish(h):
        def out_entry(i, carry):
            scale = scale2_in_s[jnp.clip(meta_ref[8, i], 0, blks - 1), 0, jnp.clip(meta_ref[9, i], 0, width - 1)] * meta_ref[12, i].astype(jnp.float32)
            mirrored = value_of(recv2[h][jnp.clip(meta_ref[10, i], 0, span // 2 - 1)], meta_ref[11, i])
            total = own[h, i] + mirrored * scale
            columns = pl.ds(pl.multiple_of(i * width, width), width)
            out_ref[h * half : (h + 1) * half, columns] = total.astype(jnp.bfloat16)
            return carry

        lax.fori_loop(0, span, out_entry, 0, unroll=unroll_of(span, 8))

    wait_products(HALVES)
    table_copy(scale1_in, scale1_s, 3).start()
    table_copy(scale1_in, scale1_s, 3).wait()

    def scale_entry(i, carry):
        scale2_s[i // glen, 0, i % glen] = scale1_s[jnp.clip(meta_ref[4, i], 0, devices - 1), 0, jnp.clip(meta_ref[5, i], 0, width - 1)]
        return carry

    lax.fori_loop(0, span, scale_entry, 0, unroll=unroll_of(span, 8))
    table_copy(scale2_s, scale2, 4).start()
    table_copy(scale2_s, scale2, 4).wait()

    @pl.loop(0, blks)
    def _(step):
        mirror_copy(HALVES, step).start()

    wait_products(0)
    gather(0)

    @pl.loop(0, blks)
    def _(step):
        mirror_copy(HALVES, step).wait()

    table_copy(scale2_in, scale2_in_s, 5).start()
    table_copy(scale2_in, scale2_in_s, 5).wait()
    wait_products(1)
    gather(1)
    for h in range(HALVES):

        @pl.loop(0, blks)
        def _(step):
            mirror_copy(h, step).wait()

        finish(h)


def local(amplitudes, integrals, block_irrep, slab_blocks, owner, partner, sign):
    rows, columns = amplitudes.shape
    slots, per_irrep, _, width = integrals.shape
    blks = lax.axis_size("blk")
    pairs = lax.axis_size("pair")
    devices = blks * pairs
    span = columns // width
    cap = slots // blks
    glen = span // blks
    slab_count = slab_blocks.shape[0]
    irreps = slab_count // per_irrep
    chunk = slab_count // blks
    inner = per_irrep * width
    capw, half = -(-cap // 2), rows // 2
    tables = [table.reshape(-1, width) for table in (owner, partner, block_irrep, sign)]

    sizes = (blks, pairs, span, cap, per_irrep, slab_count, rows, width)
    smem = pl.BlockSpec(memory_space=pltpu.SMEM)
    vmem = pl.BlockSpec(memory_space=pltpu.VMEM)
    dma = pltpu.SemaphoreType.DMA
    hbm = pl.BlockSpec(memory_space=pl.ANY)
    return pl.pallas_call(
        functools.partial(kernel, sizes),
        out_shape=jax.ShapeDtypeStruct((rows, columns), jnp.bfloat16),
        in_specs=[smem] + [vmem] * 4 + [hbm, hbm],
        out_specs=vmem,
        scratch_shapes=[
            pltpu.VMEM((rows, columns), jnp.bfloat16),
            pltpu.VMEM((span, rows, width), jnp.bfloat16),
            pltpu.VMEM((slab_count, rows, width), jnp.bfloat16),
            pltpu.VMEM((blks, width), jnp.int32),
            pltpu.VMEM((16, span), jnp.int32),
            pltpu.SMEM((blks, width), jnp.int32),
            pltpu.SMEM((16, span), jnp.int32),
            pltpu.VMEM((slots, inner, width), jnp.bfloat16),
            pltpu.VMEM((blks, chunk, rows, width), jnp.bfloat16),
            pltpu.VMEM((pairs, blks, chunk, rows, width), jnp.bfloat16),
            pltpu.VMEM((irreps, rows * pairs, inner), jnp.bfloat16),
            *[pltpu.VMEM((devices * capw, half, width), jnp.int32)] * 4,
            pltpu.VMEM((devices, 1, width), jnp.float32),
            pltpu.VMEM((devices, 1, width), jnp.float32),
            pltpu.SMEM((devices, 1, width), jnp.float32),
            pltpu.VMEM((HALVES, span, half, width), jnp.float32),
            *[pltpu.VMEM((span // 2, half, width), jnp.int32)] * 4,
            pltpu.SMEM((blks, 1, width), jnp.float32),
            pltpu.VMEM((blks, 1, width), jnp.float32),
            pltpu.VMEM((blks, 1, width), jnp.float32),
            pltpu.SMEM((blks, 1, width), jnp.float32),
            dma((blks,)),
            dma((blks,)),
            dma((blks,)),
            dma((blks,)),
            dma((blks,)),
            dma((blks, pairs)),
            dma((blks, pairs)),
            dma((HALVES + 1, blks, pairs)),
            dma((HALVES + 1, blks, pairs)),
            dma((HALVES + 1, blks)),
            dma((HALVES + 1, blks)),
            dma((6,)),
        ],
        compiler_params=pltpu.CompilerParams(
            collective_id=0, has_side_effects=True, vmem_limit_bytes=56 * 2**20
        ),
    )(
        slab_blocks,
        *tables,
        amplitudes,
        integrals.reshape(slots, inner, width),
    )


def solution(mesh):
    placed = (P("pair", "blk"), P(("blk", "pair"), None, None, None), P(), P(), P(), P(), P())
    return jax.shard_map(
        local, mesh=mesh, in_specs=placed, out_specs=P("pair", "blk"), check_vma=False
    )
```

```python
import functools

import jax
import jax.numpy as jnp
from jax import lax
from jax.experimental import pallas as pl
from jax.experimental.pallas import tpu as pltpu
from jax.sharding import PartitionSpec as P

TOP = 32766.0
TINY = 2.0**-110
MESH = pl.DeviceIdType.MESH
HALVES = 2


def unroll_of(trips, most):
    return max(n for n in range(1, most + 1) if trips % n == 0)


def fill_tables(sizes, owner_ref, partner_ref, irrep_ref, sign_ref, irrep_out, meta_out):
    blks, pairs, span, cap, per_irrep, slab_count, rows, width = sizes
    me_blk = lax.axis_index("blk")
    me = me_blk * pairs + lax.axis_index("pair")

    down = lax.broadcasted_iota(jnp.int32, (span, span), 0)
    across = lax.broadcasted_iota(jnp.int32, (span, span), 1)
    diagonal = down == across
    earlier = down < across

    def column(row):
        return jnp.sum(jnp.where(diagonal, row, 0.0), axis=1, keepdims=True)

    def count(mask):
        return jnp.sum(jnp.where(mask, 1.0, 0.0), axis=0, keepdims=True)

    def placed(keys, values):
        hit = keys == across.astype(jnp.float32)
        return jnp.sum(jnp.where(hit, values, 0.0), axis=0, keepdims=True)

    parts = span // width

    def mine(ref):
        found = [ref[pl.ds(me_blk * parts + part, 1), :] for part in range(parts)]
        return jnp.concatenate(found, axis=1).astype(jnp.float32)

    def every(ref):
        found = [
            jnp.concatenate([ref[b * parts + part : b * parts + part + 1, :] for b in range(blks)])
            for part in range(parts)
        ]
        return jnp.concatenate(found, axis=1)

    owner, partner, sign = mine(owner_ref), mine(partner_ref), mine(sign_ref)
    partner_blk = jnp.floor((partner + 0.5) * (1.0 / span))
    owner_col, partner_col, blk_col = column(owner), column(partner), column(partner_blk)
    same_blk = blk_col == partner_blk
    rank = count(jnp.logical_and(owner_col == owner, earlier))
    send_key = partner_blk * (span // blks) + count(jnp.logical_and(same_blk, earlier))
    mirror_rank = count(jnp.logical_and(same_blk, partner_col < partner))
    key_col = column(send_key)
    send_dev = placed(key_col, owner_col)
    send_rank = placed(key_col, column(rank))
    capw, glenw = -(-cap // 2), span // blks // 2
    table = []
    for index, most, count_of, place in (
        (owner, blks * pairs, capw, rank),
        (send_dev, blks * pairs, capw, send_rank),
        (partner_blk, blks, glenw, mirror_rank),
    ):
        index = jnp.clip(index, 0.0, most - 1.0)
        place = jnp.clip(place, 0.0, min(2 * count_of, width) - 1.0)
        word = jnp.floor(place * 0.5)
        shift = 16.0 - 16.0 * (place - 2.0 * word)
        table += [index, place, index * count_of + word, shift]
    for at, row in enumerate(table + [sign]):
        meta_out[at : at + 1, :] = row.astype(jnp.int32)

    stored = every(owner_ref) == me
    ranks = jnp.dot(
        jnp.where(stored, 1.0, 0.0).astype(jnp.bfloat16),
        jnp.where(earlier, 1.0, 0.0).astype(jnp.bfloat16),
        preferred_element_type=jnp.float32,
    ).astype(jnp.int32)
    ranks = jnp.where(stored, ranks, -1)
    irrep = every(irrep_ref).astype(jnp.float32)
    lane = lax.broadcasted_iota(jnp.int32, (blks, width), 1)
    slots = jnp.zeros((blks, width), jnp.float32)
    for r in range(cap):
        found = jnp.sum(jnp.where(ranks == r, irrep, 0.0), axis=1, keepdims=True)
        slots = jnp.where(lane == r, found, slots)
    irrep_out[...] = slots.astype(jnp.int32)


def kernel(
    sizes,
    slab_ref,
    owner_ref,
    partner_ref,
    irreps_ref,
    sign_ref,
    amp_hbm,
    ints_hbm,
    out_ref,
    amp,
    amp_blocks,
    picked,
    irrep_v,
    meta_v,
    irrep_ref,
    meta_ref,
    ints,
    picked_in,
    slab_in,
    slab,
    send1a,
    send1b,
    recv1a,
    recv1b,
    scale1,
    scale1_in,
    scale1_s,
    own,
    send2a,
    send2b,
    recv2a,
    recv2b,
    scale2_s,
    scale2,
    scale2_in,
    scale2_in_s,
    factor_s,
    ints_sem,
    pick_send,
    pick_recv,
    gath_send,
    gath_recv,
    fwd_send,
    fwd_recv,
    send1_sem,
    recv1_sem,
    send2_sem,
    recv2_sem,
    table_sem,
):
    blks, pairs, span, cap, per_irrep, slab_count, rows, width = sizes
    devices = blks * pairs
    chunk = slab_count // blks
    glen = span // blks
    me_blk = lax.axis_index("blk")
    me_pair = lax.axis_index("pair")
    me = me_blk * pairs + me_pair
    capw, glenw, half = -(-cap // 2), glen // 2, rows // 2
    lane = lax.broadcasted_iota(jnp.int32, (1, width), 1)
    send1, recv1 = (send1a, send1b), (recv1a, recv1b)
    send2, recv2 = (send2a, send2b), (recv2a, recv2b)

    def blk_at(step):
        pattern = blks // 2 + (1 - step % 2) * (step // 2) - (step % 2) * ((step + 1) // 2)
        found, bit = 0, 1
        while bit < blks:
            found = found + lax.rem(me_blk // bit + pattern // bit, 2) * bit
            bit *= 2
        return found

    def ints_copy(step):
        at = blk_at(step)
        return pltpu.make_async_copy(
            ints_hbm.at[pl.ds(at * cap, cap)], ints.at[pl.ds(at * cap, cap)], ints_sem.at[step]
        )

    def table_copy(source, target, at):
        return pltpu.make_async_copy(source, target, table_sem.at[at])

    table_copy(amp_hbm, amp, 0).start()

    @pl.loop(0, blks)
    def _(step):
        ints_copy(step).start()

    barrier = pltpu.get_barrier_semaphore()

    @pl.loop(1, devices)
    def _(step):
        other = lax.rem(me + step, devices)
        pl.semaphore_signal(
            barrier,
            inc=1,
            device_id={"blk": other // pairs, "pair": lax.rem(other, pairs)},
            device_id_type=MESH,
        )

    table_copy(amp_hbm, amp, 0).wait()

    def split(i, carry):
        amp_blocks[i] = amp[:, pl.ds(pl.multiple_of(i * width, width), width)]
        return carry

    lax.fori_loop(0, span, split, 0, unroll=unroll_of(span, 8))
    for n in range(slab_count):
        local = slab_ref[n] - me_blk * span
        inside = jnp.logical_and(local >= 0, local < span).astype(jnp.float32)
        block = amp_blocks[jnp.clip(local, 0, span - 1)]
        picked[n] = (block.astype(jnp.float32) * inside).astype(jnp.bfloat16)

    pl.semaphore_wait(barrier, devices - 1)

    def pick_copy(step):
        to = blk_at(step)
        return pltpu.make_async_remote_copy(
            src_ref=picked.at[pl.ds(to * chunk, chunk)],
            dst_ref=picked_in.at[me_blk],
            send_sem=pick_send.at[step],
            recv_sem=pick_recv.at[step],
            device_id={"blk": to},
            device_id_type=MESH,
        )

    @pl.loop(0, blks - 1)
    def _(step):
        pick_copy(step).start()

    fill_tables(sizes, owner_ref, partner_ref, irreps_ref, sign_ref, irrep_v, meta_v)
    table_copy(irrep_v, irrep_ref, 1).start()
    table_copy(meta_v, meta_ref, 2).start()

    @pl.loop(0, blks - 1)
    def _(step):
        pick_copy(step).wait()

    total = picked[pl.ds(me_blk * chunk, chunk)].astype(jnp.float32)
    for step in range(blks - 1):
        total = total + picked_in[blk_at(step)].astype(jnp.float32)
    slab_in[me_pair, me_blk] = total.astype(jnp.bfloat16)

    def gath_copy(step):
        return pltpu.make_async_remote_copy(
            src_ref=slab_in.at[me_pair, me_blk],
            dst_ref=slab_in.at[me_pair, me_blk],
            send_sem=gath_send.at[step],
            recv_sem=gath_recv.at[step],
            device_id={"blk": blk_at(step)},
            device_id_type=MESH,
        )

    def fwd_copy(source_blk, step, turn):
        return pltpu.make_async_remote_copy(
            src_ref=slab_in.at[me_pair, source_blk],
            dst_ref=slab_in.at[me_pair, source_blk],
            send_sem=fwd_send.at[step, turn],
            recv_sem=fwd_recv.at[step, turn],
            device_id={"pair": lax.rem(me_pair + 1 + turn, pairs)},
            device_id_type=MESH,
        )

    @pl.loop(0, blks - 1)
    def _(step):
        gath_copy(step).start()

    for turn in range(pairs - 1):
        fwd_copy(me_blk, blks - 1, turn).start()


    @pl.loop(0, blks - 1)
    def _(step):
        gath_copy(step).wait_recv()
        for turn in range(pairs - 1):
            fwd_copy(blk_at(step), step, turn).start()

    table_copy(irrep_v, irrep_ref, 1).wait()
    table_copy(meta_v, meta_ref, 2).wait()

    def pair_at(turn):
        return lax.rem(me_pair + turn, pairs)

    def fill_slab(turns):
        for n in range(slab_count):
            columns = slice((n % per_irrep) * width, (n % per_irrep + 1) * width)
            for turn in turns:
                place = slice(turn * rows, (turn + 1) * rows)
                slab[n // per_irrep, place, columns] = slab_in[pair_at(turn), n // chunk, n % chunk]

    def products(to, turns):
        low, high = turns[0] * rows, (turns[-1] + 1) * rows

        def slots(j, scales):
            coded = []
            for turn in range(2):
                r = jnp.minimum(2 * j + turn, cap - 1)
                product = jnp.dot(
                    slab[jnp.clip(irrep_ref[to, r], 0, slab_count // per_irrep - 1), low:high],
                    ints[to * cap + r],
                    preferred_element_type=jnp.float32,
                )
                tiles, found = [], []
                for p in range(len(turns)):
                    tile = product[p * rows : (p + 1) * rows]
                    largest = jnp.max(jnp.abs(tile), axis=0, keepdims=True)
                    largest = jnp.maximum(jnp.max(largest, axis=1, keepdims=True), TINY)
                    tiles.append(jnp.round(tile * (TOP / largest)).astype(jnp.int32))
                    found.append(jnp.where(lane == r, largest * (1.0 / TOP), scales[p]))
                scales = tuple(found)
                coded.append(tiles)
            for p in range(len(turns)):
                word = (coded[0][p] & 0xFFFF) | (coded[1][p] << 16)
                for h in range(HALVES):
                    send1[h][(to * pairs + pair_at(turns[p])) * capw + j] = word[h * half : (h + 1) * half]
            return scales

        start = tuple(jnp.zeros((1, width), jnp.float32) for _ in turns)
        scales = lax.fori_loop(0, capw, slots, start, unroll=unroll_of(capw, 5))
        for p in range(len(turns)):
            scale1[to * pairs + pair_at(turns[p])] = scales[p]

    def product_copy(h, step, turn):
        to = blk_at(step)
        to_pair = lax.rem(me_pair + turn, pairs)
        at = to * pairs + to_pair
        if h == HALVES:
            source, target = scale1.at[at], scale1_in.at[me]
        else:
            source = send1[h].at[pl.ds(at * capw, capw)]
            target = recv1[h].at[pl.ds(me * capw, capw)]
        return pltpu.make_async_remote_copy(
            src_ref=source,
            dst_ref=target,
            send_sem=send1_sem.at[h, step, turn],
            recv_sem=recv1_sem.at[h, step, turn],
            device_id={"blk": to, "pair": to_pair},
            device_id_type=MESH,
        )

    def keep_copy(h):
        if h == HALVES:
            source, target = scale1.at[me], scale1_in.at[me]
        else:
            source = send1[h].at[pl.ds(me * capw, capw)]
            target = recv1[h].at[pl.ds(me * capw, capw)]
        return pltpu.make_async_copy(source, target, send1_sem.at[h, blks - 1, 0])

    def send_products(h):
        for turn in range(1, pairs):
            product_copy(h, 0, turn).start()

        @pl.loop(1, blks - 1)
        def _(step):
            for turn in range(pairs):
                product_copy(h, step, turn).start()

        keep_copy(h).start()
        for turn in range(1, pairs):
            product_copy(h, blks - 1, turn).start()

    def wait_products(h):
        keep_copy(h).wait()

        @pl.loop(0, blks - 1)
        def _(step):
            for turn in range(pairs):
                product_copy(h, step, turn).wait()

        for turn in range(1, pairs):
            product_copy(h, blks - 1, turn).wait()

    ints_copy(0).wait()
    fill_slab([0])
    products(blk_at(0), [0])
    for h in (HALVES, 0, 1):
        product_copy(h, 0, 0).start()

    @pl.loop(0, blks - 1)
    def _(step):
        gath_copy(step).wait_send()

    @pl.loop(0, blks)
    def _(step):
        for turn in range(pairs - 1):
            fwd_copy(blk_at(step), step, turn).wait()

    every_turn = list(range(pairs))
    fill_slab(every_turn[1:])
    products(blk_at(0), every_turn[1:])
    for h in (HALVES, 0):
        for turn in range(1, pairs):
            product_copy(h, 0, turn).start()

    @pl.loop(1, blks - 1)
    def _(step):
        ints_copy(step).wait()
        products(blk_at(step), every_turn)
        for h in (HALVES, 0):
            for turn in range(pairs):
                product_copy(h, step, turn).start()

    ints_copy(blks - 1).wait()
    products(me_blk, every_turn)
    for h in (HALVES, 0):
        keep_copy(h).start()
        for turn in range(1, pairs):
            product_copy(h, blks - 1, turn).start()
    send_products(1)

    def mirror_copy(h, step):
        to = blk_at(step)
        if h == HALVES:
            source, target = scale2.at[to], scale2_in.at[me_blk]
        else:
            source = send2[h].at[pl.ds(to * glenw, glenw)]
            target = recv2[h].at[pl.ds(me_blk * glenw, glenw)]
        return pltpu.make_async_remote_copy(
            src_ref=source,
            dst_ref=target,
            send_sem=send2_sem.at[h, step],
            recv_sem=recv2_sem.at[h, step],
            device_id={"blk": to, "pair": lax.rem(me_pair + pairs // 2, pairs)},
            device_id_type=MESH,
        )

    def value_of(word, shift):
        return ((word << shift) >> 16).astype(jnp.float32)

    def gather(h):
        @pl.loop(0, blks)
        def _(step):
            to = blk_at(step)

            def entry(m, carry):
                i = to * glen + 2 * m
                low = recv1[h][jnp.clip(meta_ref[6, i], 0, devices * capw - 1)] << meta_ref[7, i]
                high = recv1[h][jnp.clip(meta_ref[6, i + 1], 0, devices * capw - 1)] << meta_ref[7, i + 1]
                send2[h][to * glenw + m] = lax.shift_right_logical(low, 16) | (high & -65536)
                return carry

            lax.fori_loop(0, glenw, entry, 0, unroll=unroll_of(glenw, 8))
            mirror_copy(h, step).start()

        def own_entry(i, carry):
            scale = scale1_s[jnp.clip(meta_ref[0, i], 0, devices - 1), 0, jnp.clip(meta_ref[1, i], 0, width - 1)]
            own[h, i] = value_of(recv1[h][jnp.clip(meta_ref[2, i], 0, devices * capw - 1)], meta_ref[3, i]) * scale
            return carry

        lax.fori_loop(0, span, own_entry, 0, unroll=unroll_of(span, 8))

    def finish(h):
        def out_entry(i, carry):
            if h == 0:
                place = (jnp.clip(meta_ref[8, i], 0, blks - 1), jnp.clip(meta_ref[9, i], 0, width - 1))
                scale = scale2_in_s[place[0], 0, place[1]] * meta_ref[12, i].astype(jnp.float32)
                factor_s[i] = scale
            else:
                scale = factor_s[i]
            mirrored = value_of(recv2[h][jnp.clip(meta_ref[10, i], 0, span // 2 - 1)], meta_ref[11, i])
            total = own[h, i] + mirrored * scale
            columns = pl.ds(pl.multiple_of(i * width, width), width)
            out_ref[h * half : (h + 1) * half, columns] = total.astype(jnp.bfloat16)
            return carry

        lax.fori_loop(0, span, out_entry, 0, unroll=unroll_of(span, 8))

    wait_products(HALVES)
    table_copy(scale1_in, scale1_s, 3).start()
    table_copy(scale1_in, scale1_s, 3).wait()

    def scale_entry(i, carry):
        scale2_s[i // glen, 0, i % glen] = scale1_s[jnp.clip(meta_ref[4, i], 0, devices - 1), 0, jnp.clip(meta_ref[5, i], 0, width - 1)]
        return carry

    lax.fori_loop(0, span, scale_entry, 0, unroll=unroll_of(span, 8))
    table_copy(scale2_s, scale2, 4).start()
    table_copy(scale2_s, scale2, 4).wait()

    @pl.loop(0, blks)
    def _(step):
        mirror_copy(HALVES, step).start()

    wait_products(0)
    gather(0)

    @pl.loop(0, blks)
    def _(step):
        mirror_copy(HALVES, step).wait()

    table_copy(scale2_in, scale2_in_s, 5).start()
    table_copy(scale2_in, scale2_in_s, 5).wait()
    wait_products(1)
    gather(1)
    for h in range(HALVES):

        @pl.loop(0, blks)
        def _(step):
            mirror_copy(h, step).wait()

        finish(h)


def local(amplitudes, integrals, block_irrep, slab_blocks, owner, partner, sign):
    rows, columns = amplitudes.shape
    slots, per_irrep, _, width = integrals.shape
    blks = lax.axis_size("blk")
    pairs = lax.axis_size("pair")
    devices = blks * pairs
    span = columns // width
    cap = slots // blks
    glen = span // blks
    slab_count = slab_blocks.shape[0]
    irreps = slab_count // per_irrep
    chunk = slab_count // blks
    inner = per_irrep * width
    capw, half = -(-cap // 2), rows // 2
    tables = [table.reshape(-1, width) for table in (owner, partner, block_irrep, sign)]

    sizes = (blks, pairs, span, cap, per_irrep, slab_count, rows, width)
    smem = pl.BlockSpec(memory_space=pltpu.SMEM)
    vmem = pl.BlockSpec(memory_space=pltpu.VMEM)
    dma = pltpu.SemaphoreType.DMA
    hbm = pl.BlockSpec(memory_space=pl.ANY)
    return pl.pallas_call(
        functools.partial(kernel, sizes),
        out_shape=jax.ShapeDtypeStruct((rows, columns), jnp.bfloat16),
        in_specs=[smem] + [vmem] * 4 + [hbm, hbm],
        out_specs=vmem,
        scratch_shapes=[
            pltpu.VMEM((rows, columns), jnp.bfloat16),
            pltpu.VMEM((span, rows, width), jnp.bfloat16),
            pltpu.VMEM((slab_count, rows, width), jnp.bfloat16),
            pltpu.VMEM((blks, width), jnp.int32),
            pltpu.VMEM((16, span), jnp.int32),
            pltpu.SMEM((blks, width), jnp.int32),
            pltpu.SMEM((16, span), jnp.int32),
            pltpu.VMEM((slots, inner, width), jnp.bfloat16),
            pltpu.VMEM((blks, chunk, rows, width), jnp.bfloat16),
            pltpu.VMEM((pairs, blks, chunk, rows, width), jnp.bfloat16),
            pltpu.VMEM((irreps, rows * pairs, inner), jnp.bfloat16),
            *[pltpu.VMEM((devices * capw, half, width), jnp.int32)] * 4,
            pltpu.VMEM((devices, 1, width), jnp.float32),
            pltpu.VMEM((devices, 1, width), jnp.float32),
            pltpu.SMEM((devices, 1, width), jnp.float32),
            pltpu.VMEM((HALVES, span, half, width), jnp.float32),
            *[pltpu.VMEM((span // 2, half, width), jnp.int32)] * 4,
            pltpu.SMEM((blks, 1, width), jnp.float32),
            pltpu.VMEM((blks, 1, width), jnp.float32),
            pltpu.VMEM((blks, 1, width), jnp.float32),
            pltpu.SMEM((blks, 1, width), jnp.float32),
            pltpu.SMEM((span,), jnp.float32),
            dma((blks,)),
            dma((blks,)),
            dma((blks,)),
            dma((blks,)),
            dma((blks,)),
            dma((blks, pairs)),
            dma((blks, pairs)),
            dma((HALVES + 1, blks, pairs)),
            dma((HALVES + 1, blks, pairs)),
            dma((HALVES + 1, blks)),
            dma((HALVES + 1, blks)),
            dma((6,)),
        ],
        compiler_params=pltpu.CompilerParams(
            collective_id=0, has_side_effects=True, vmem_limit_bytes=56 * 2**20
        ),
    )(
        slab_blocks,
        *tables,
        amplitudes,
        integrals.reshape(slots, inner, width),
    )


def solution(mesh):
    placed = (P("pair", "blk"), P(("blk", "pair"), None, None, None), P(), P(), P(), P(), P())
    return jax.shard_map(
        local, mesh=mesh, in_specs=placed, out_specs=P("pair", "blk"), check_vma=False
    )
```

```python
import functools

import jax
import jax.numpy as jnp
from jax import lax
from jax.experimental import pallas as pl
from jax.experimental.pallas import tpu as pltpu
from jax.sharding import PartitionSpec as P

TOP = 32766.0
TINY = 2.0**-110
MESH = pl.DeviceIdType.MESH
HALVES = 2


def unroll_of(trips, most):
    return max(n for n in range(1, most + 1) if trips % n == 0)


def fill_tables(sizes, owner_ref, partner_ref, irrep_ref, sign_ref, irrep_out, meta_out):
    blks, pairs, span, cap, per_irrep, slab_count, rows, width = sizes
    me_blk = lax.axis_index("blk")
    me = me_blk * pairs + lax.axis_index("pair")

    down = lax.broadcasted_iota(jnp.int32, (span, span), 0)
    across = lax.broadcasted_iota(jnp.int32, (span, span), 1)
    diagonal = down == across
    earlier = down < across

    def column(row):
        return jnp.sum(jnp.where(diagonal, row, 0.0), axis=1, keepdims=True)

    def count(mask):
        return jnp.sum(jnp.where(mask, 1.0, 0.0), axis=0, keepdims=True)

    def placed(keys, values):
        hit = keys == across.astype(jnp.float32)
        return jnp.sum(jnp.where(hit, values, 0.0), axis=0, keepdims=True)

    parts = span // width

    def mine(ref):
        found = [ref[pl.ds(me_blk * parts + part, 1), :] for part in range(parts)]
        return jnp.concatenate(found, axis=1).astype(jnp.float32)

    def every(ref):
        found = [
            jnp.concatenate([ref[b * parts + part : b * parts + part + 1, :] for b in range(blks)])
            for part in range(parts)
        ]
        return jnp.concatenate(found, axis=1)

    owner, partner, sign = mine(owner_ref), mine(partner_ref), mine(sign_ref)
    partner_blk = jnp.floor((partner + 0.5) * (1.0 / span))
    owner_col, partner_col, blk_col = column(owner), column(partner), column(partner_blk)
    same_blk = blk_col == partner_blk
    rank = count(jnp.logical_and(owner_col == owner, earlier))
    send_key = partner_blk * (span // blks) + count(jnp.logical_and(same_blk, earlier))
    mirror_rank = count(jnp.logical_and(same_blk, partner_col < partner))
    key_col = column(send_key)
    send_dev = placed(key_col, owner_col)
    send_rank = placed(key_col, column(rank))
    capw, glenw = -(-cap // 2), span // blks // 2
    table = []
    for index, most, count_of, place in (
        (owner, blks * pairs, capw, rank),
        (send_dev, blks * pairs, capw, send_rank),
        (partner_blk, blks, glenw, mirror_rank),
    ):
        index = jnp.clip(index, 0.0, most - 1.0)
        place = jnp.clip(place, 0.0, min(2 * count_of, width) - 1.0)
        word = jnp.floor(place * 0.5)
        shift = 16.0 - 16.0 * (place - 2.0 * word)
        table += [index, place, index * count_of + word, shift]
    for at, row in enumerate(table + [sign]):
        meta_out[at : at + 1, :] = row.astype(jnp.int32)

    stored = every(owner_ref) == me
    ranks = jnp.dot(
        jnp.where(stored, 1.0, 0.0).astype(jnp.bfloat16),
        jnp.where(earlier, 1.0, 0.0).astype(jnp.bfloat16),
        preferred_element_type=jnp.float32,
    ).astype(jnp.int32)
    ranks = jnp.where(stored, ranks, -1)
    irrep = every(irrep_ref).astype(jnp.float32)
    lane = lax.broadcasted_iota(jnp.int32, (blks, width), 1)
    slots = jnp.zeros((blks, width), jnp.float32)
    for r in range(cap):
        found = jnp.sum(jnp.where(ranks == r, irrep, 0.0), axis=1, keepdims=True)
        slots = jnp.where(lane == r, found, slots)
    irrep_out[...] = slots.astype(jnp.int32)


def kernel(
    sizes,
    slab_ref,
    owner_ref,
    partner_ref,
    irreps_ref,
    sign_ref,
    amp_hbm,
    ints_hbm,
    out_ref,
    amp,
    amp_blocks,
    picked,
    irrep_v,
    meta_v,
    irrep_ref,
    meta_ref,
    ints,
    picked_in,
    slab_in,
    slab,
    send1a,
    send1b,
    recv1a,
    recv1b,
    scale1,
    scale1_in,
    scale1_s,
    own,
    send2a,
    send2b,
    recv2a,
    recv2b,
    scale2_s,
    scale2,
    scale2_in,
    scale2_in_s,
    factor_s,
    ints_sem,
    pick_send,
    pick_recv,
    gath_send,
    gath_recv,
    fwd_send,
    fwd_recv,
    send1_sem,
    recv1_sem,
    send2_sem,
    recv2_sem,
    table_sem,
):
    blks, pairs, span, cap, per_irrep, slab_count, rows, width = sizes
    devices = blks * pairs
    chunk = slab_count // blks
    glen = span // blks
    me_blk = lax.axis_index("blk")
    me_pair = lax.axis_index("pair")
    me = me_blk * pairs + me_pair
    capw, glenw, half = -(-cap // 2), glen // 2, rows // 2
    lane = lax.broadcasted_iota(jnp.int32, (1, width), 1)
    send1, recv1 = (send1a, send1b), (recv1a, recv1b)
    send2, recv2 = (send2a, send2b), (recv2a, recv2b)

    def blk_at(step):
        pattern = blks // 2 + (1 - step % 2) * (step // 2) - (step % 2) * ((step + 1) // 2)
        found, bit = 0, 1
        while bit < blks:
            found = found + lax.rem(me_blk // bit + pattern // bit, 2) * bit
            bit *= 2
        return found

    def ints_copy(step):
        at = blk_at(step)
        return pltpu.make_async_copy(
            ints_hbm.at[pl.ds(at * cap, cap)], ints.at[pl.ds(at * cap, cap)], ints_sem.at[step]
        )

    def table_copy(source, target, at):
        return pltpu.make_async_copy(source, target, table_sem.at[at])

    table_copy(amp_hbm, amp, 0).start()

    @pl.loop(0, blks)
    def _(step):
        ints_copy(step).start()

    barrier = pltpu.get_barrier_semaphore()

    @pl.loop(0, blks - 1)
    def _(step):
        pl.semaphore_signal(barrier, inc=1, device_id={"blk": blk_at(step)}, device_id_type=MESH)

    for turn in range(1, pairs):
        pl.semaphore_signal(
            barrier, inc=1, device_id={"pair": lax.rem(me_pair + turn, pairs)}, device_id_type=MESH
        )

    table_copy(amp_hbm, amp, 0).wait()

    def split(i, carry):
        amp_blocks[i] = amp[:, pl.ds(pl.multiple_of(i * width, width), width)]
        return carry

    lax.fori_loop(0, span, split, 0, unroll=unroll_of(span, 8))
    for n in range(slab_count):
        local = slab_ref[n] - me_blk * span
        inside = jnp.logical_and(local >= 0, local < span).astype(jnp.float32)
        block = amp_blocks[jnp.clip(local, 0, span - 1)]
        picked[n] = (block.astype(jnp.float32) * inside).astype(jnp.bfloat16)

    pl.semaphore_wait(barrier, blks + pairs - 2)

    def pick_copy(step):
        to = blk_at(step)
        return pltpu.make_async_remote_copy(
            src_ref=picked.at[pl.ds(to * chunk, chunk)],
            dst_ref=picked_in.at[me_blk],
            send_sem=pick_send.at[step],
            recv_sem=pick_recv.at[step],
            device_id={"blk": to},
            device_id_type=MESH,
        )

    @pl.loop(0, blks - 1)
    def _(step):
        pick_copy(step).start()

    fill_tables(sizes, owner_ref, partner_ref, irreps_ref, sign_ref, irrep_v, meta_v)
    table_copy(irrep_v, irrep_ref, 1).start()
    table_copy(meta_v, meta_ref, 2).start()

    @pl.loop(0, blks - 1)
    def _(step):
        pick_copy(step).wait()

    total = picked[pl.ds(me_blk * chunk, chunk)].astype(jnp.float32)
    for step in range(blks - 1):
        total = total + picked_in[blk_at(step)].astype(jnp.float32)
    slab_in[me_pair, me_blk] = total.astype(jnp.bfloat16)

    def gath_copy(step):
        return pltpu.make_async_remote_copy(
            src_ref=slab_in.at[me_pair, me_blk],
            dst_ref=slab_in.at[me_pair, me_blk],
            send_sem=gath_send.at[step],
            recv_sem=gath_recv.at[step],
            device_id={"blk": blk_at(step)},
            device_id_type=MESH,
        )

    def fwd_copy(source_blk, step, turn):
        return pltpu.make_async_remote_copy(
            src_ref=slab_in.at[me_pair, source_blk],
            dst_ref=slab_in.at[me_pair, source_blk],
            send_sem=fwd_send.at[step, turn],
            recv_sem=fwd_recv.at[step, turn],
            device_id={"pair": lax.rem(me_pair + 1 + turn, pairs)},
            device_id_type=MESH,
        )

    @pl.loop(0, blks - 1)
    def _(step):
        gath_copy(step).start()

    for turn in range(pairs - 1):
        fwd_copy(me_blk, blks - 1, turn).start()


    @pl.loop(0, blks - 1)
    def _(step):
        gath_copy(step).wait_recv()
        for turn in range(pairs - 1):
            fwd_copy(blk_at(step), step, turn).start()

    table_copy(irrep_v, irrep_ref, 1).wait()
    table_copy(meta_v, meta_ref, 2).wait()

    def pair_at(turn):
        return lax.rem(me_pair + turn, pairs)

    def fill_slab(turns):
        for n in range(slab_count):
            columns = slice((n % per_irrep) * width, (n % per_irrep + 1) * width)
            for turn in turns:
                place = slice(turn * rows, (turn + 1) * rows)
                slab[n // per_irrep, place, columns] = slab_in[pair_at(turn), n // chunk, n % chunk]

    def products(to, turns):
        low, high = turns[0] * rows, (turns[-1] + 1) * rows

        def slots(j, scales):
            coded = []
            for turn in range(2):
                r = jnp.minimum(2 * j + turn, cap - 1)
                product = jnp.dot(
                    slab[jnp.clip(irrep_ref[to, r], 0, slab_count // per_irrep - 1), low:high],
                    ints[to * cap + r],
                    preferred_element_type=jnp.float32,
                )
                tiles, found = [], []
                for p in range(len(turns)):
                    tile = product[p * rows : (p + 1) * rows]
                    largest = jnp.max(jnp.abs(tile), axis=0, keepdims=True)
                    largest = jnp.maximum(jnp.max(largest, axis=1, keepdims=True), TINY)
                    tiles.append(jnp.round(tile * (TOP / largest)).astype(jnp.int32))
                    found.append(jnp.where(lane == r, largest * (1.0 / TOP), scales[p]))
                scales = tuple(found)
                coded.append(tiles)
            for p in range(len(turns)):
                word = (coded[0][p] & 0xFFFF) | (coded[1][p] << 16)
                for h in range(HALVES):
                    send1[h][(to * pairs + pair_at(turns[p])) * capw + j] = word[h * half : (h + 1) * half]
            return scales

        start = tuple(jnp.zeros((1, width), jnp.float32) for _ in turns)
        scales = lax.fori_loop(0, capw, slots, start, unroll=unroll_of(capw, 5))
        for p in range(len(turns)):
            scale1[to * pairs + pair_at(turns[p])] = scales[p]

    def product_copy(h, step, turn):
        to = blk_at(step)
        to_pair = lax.rem(me_pair + turn, pairs)
        at = to * pairs + to_pair
        if h == HALVES:
            source, target = scale1.at[at], scale1_in.at[me]
        else:
            source = send1[h].at[pl.ds(at * capw, capw)]
            target = recv1[h].at[pl.ds(me * capw, capw)]
        return pltpu.make_async_remote_copy(
            src_ref=source,
            dst_ref=target,
            send_sem=send1_sem.at[h, step, turn],
            recv_sem=recv1_sem.at[h, step, turn],
            device_id={"blk": to, "pair": to_pair},
            device_id_type=MESH,
        )

    def keep_copy(h):
        if h == HALVES:
            source, target = scale1.at[me], scale1_in.at[me]
        else:
            source = send1[h].at[pl.ds(me * capw, capw)]
            target = recv1[h].at[pl.ds(me * capw, capw)]
        return pltpu.make_async_copy(source, target, send1_sem.at[h, blks - 1, 0])

    def send_products(h):
        for turn in range(1, pairs):
            product_copy(h, 0, turn).start()

        @pl.loop(1, blks - 1)
        def _(step):
            for turn in range(pairs):
                product_copy(h, step, turn).start()

        keep_copy(h).start()
        for turn in range(1, pairs):
            product_copy(h, blks - 1, turn).start()

    def wait_products(h):
        keep_copy(h).wait()

        @pl.loop(0, blks - 1)
        def _(step):
            for turn in range(pairs):
                product_copy(h, step, turn).wait()

        for turn in range(1, pairs):
            product_copy(h, blks - 1, turn).wait()

    ints_copy(0).wait()
    fill_slab([0])
    products(blk_at(0), [0])
    for h in (HALVES, 0, 1):
        product_copy(h, 0, 0).start()

    @pl.loop(0, blks - 1)
    def _(step):
        gath_copy(step).wait_send()

    @pl.loop(0, blks)
    def _(step):
        for turn in range(pairs - 1):
            fwd_copy(blk_at(step), step, turn).wait()

    every_turn = list(range(pairs))
    fill_slab(every_turn[1:])
    products(blk_at(0), every_turn[1:])
    for h in (HALVES, 0):
        for turn in range(1, pairs):
            product_copy(h, 0, turn).start()

    @pl.loop(1, blks - 1)
    def _(step):
        ints_copy(step).wait()
        products(blk_at(step), every_turn)
        for h in (HALVES, 0):
            for turn in range(pairs):
                product_copy(h, step, turn).start()

    ints_copy(blks - 1).wait()
    products(me_blk, every_turn)
    for h in (HALVES, 0):
        keep_copy(h).start()
        for turn in range(1, pairs):
            product_copy(h, blks - 1, turn).start()
    send_products(1)

    def mirror_copy(h, step):
        to = blk_at(step)
        if h == HALVES:
            source, target = scale2.at[to], scale2_in.at[me_blk]
        else:
            source = send2[h].at[pl.ds(to * glenw, glenw)]
            target = recv2[h].at[pl.ds(me_blk * glenw, glenw)]
        return pltpu.make_async_remote_copy(
            src_ref=source,
            dst_ref=target,
            send_sem=send2_sem.at[h, step],
            recv_sem=recv2_sem.at[h, step],
            device_id={"blk": to, "pair": lax.rem(me_pair + pairs // 2, pairs)},
            device_id_type=MESH,
        )

    def value_of(word, shift):
        return ((word << shift) >> 16).astype(jnp.float32)

    def gather(h):
        @pl.loop(0, blks)
        def _(step):
            to = blk_at(step)

            def entry(m, carry):
                i = to * glen + 2 * m
                low = recv1[h][jnp.clip(meta_ref[6, i], 0, devices * capw - 1)] << meta_ref[7, i]
                high = recv1[h][jnp.clip(meta_ref[6, i + 1], 0, devices * capw - 1)] << meta_ref[7, i + 1]
                send2[h][to * glenw + m] = lax.shift_right_logical(low, 16) | (high & -65536)
                return carry

            lax.fori_loop(0, glenw, entry, 0, unroll=unroll_of(glenw, 8))
            mirror_copy(h, step).start()

        def own_entry(i, carry):
            scale = scale1_s[jnp.clip(meta_ref[0, i], 0, devices - 1), 0, jnp.clip(meta_ref[1, i], 0, width - 1)]
            own[h, i] = value_of(recv1[h][jnp.clip(meta_ref[2, i], 0, devices * capw - 1)], meta_ref[3, i]) * scale
            return carry

        lax.fori_loop(0, span, own_entry, 0, unroll=unroll_of(span, 8))

    def finish(h):
        def out_entry(i, carry):
            if h == 0:
                place = (jnp.clip(meta_ref[8, i], 0, blks - 1), jnp.clip(meta_ref[9, i], 0, width - 1))
                scale = scale2_in_s[place[0], 0, place[1]] * meta_ref[12, i].astype(jnp.float32)
                factor_s[i] = scale
            else:
                scale = factor_s[i]
            mirrored = value_of(recv2[h][jnp.clip(meta_ref[10, i], 0, span // 2 - 1)], meta_ref[11, i])
            total = own[h, i] + mirrored * scale
            columns = pl.ds(pl.multiple_of(i * width, width), width)
            out_ref[h * half : (h + 1) * half, columns] = total.astype(jnp.bfloat16)
            return carry

        lax.fori_loop(0, span, out_entry, 0, unroll=unroll_of(span, 8))

    wait_products(HALVES)
    table_copy(scale1_in, scale1_s, 3).start()
    table_copy(scale1_in, scale1_s, 3).wait()

    def scale_entry(i, carry):
        scale2_s[i // glen, 0, i % glen] = scale1_s[jnp.clip(meta_ref[4, i], 0, devices - 1), 0, jnp.clip(meta_ref[5, i], 0, width - 1)]
        return carry

    lax.fori_loop(0, span, scale_entry, 0, unroll=unroll_of(span, 8))
    table_copy(scale2_s, scale2, 4).start()
    table_copy(scale2_s, scale2, 4).wait()

    @pl.loop(0, blks)
    def _(step):
        mirror_copy(HALVES, step).start()

    wait_products(0)
    gather(0)

    @pl.loop(0, blks)
    def _(step):
        mirror_copy(HALVES, step).wait()

    table_copy(scale2_in, scale2_in_s, 5).start()
    table_copy(scale2_in, scale2_in_s, 5).wait()
    wait_products(1)
    gather(1)
    for h in range(HALVES):

        @pl.loop(0, blks)
        def _(step):
            mirror_copy(h, step).wait()

        finish(h)


def local(amplitudes, integrals, block_irrep, slab_blocks, owner, partner, sign):
    rows, columns = amplitudes.shape
    slots, per_irrep, _, width = integrals.shape
    blks = lax.axis_size("blk")
    pairs = lax.axis_size("pair")
    devices = blks * pairs
    span = columns // width
    cap = slots // blks
    glen = span // blks
    slab_count = slab_blocks.shape[0]
    irreps = slab_count // per_irrep
    chunk = slab_count // blks
    inner = per_irrep * width
    capw, half = -(-cap // 2), rows // 2
    tables = [table.reshape(-1, width) for table in (owner, partner, block_irrep, sign)]

    sizes = (blks, pairs, span, cap, per_irrep, slab_count, rows, width)
    smem = pl.BlockSpec(memory_space=pltpu.SMEM)
    vmem = pl.BlockSpec(memory_space=pltpu.VMEM)
    dma = pltpu.SemaphoreType.DMA
    hbm = pl.BlockSpec(memory_space=pl.ANY)
    return pl.pallas_call(
        functools.partial(kernel, sizes),
        out_shape=jax.ShapeDtypeStruct((rows, columns), jnp.bfloat16),
        in_specs=[smem] + [vmem] * 4 + [hbm, hbm],
        out_specs=vmem,
        scratch_shapes=[
            pltpu.VMEM((rows, columns), jnp.bfloat16),
            pltpu.VMEM((span, rows, width), jnp.bfloat16),
            pltpu.VMEM((slab_count, rows, width), jnp.bfloat16),
            pltpu.VMEM((blks, width), jnp.int32),
            pltpu.VMEM((16, span), jnp.int32),
            pltpu.SMEM((blks, width), jnp.int32),
            pltpu.SMEM((16, span), jnp.int32),
            pltpu.VMEM((slots, inner, width), jnp.bfloat16),
            pltpu.VMEM((blks, chunk, rows, width), jnp.bfloat16),
            pltpu.VMEM((pairs, blks, chunk, rows, width), jnp.bfloat16),
            pltpu.VMEM((irreps, rows * pairs, inner), jnp.bfloat16),
            *[pltpu.VMEM((devices * capw, half, width), jnp.int32)] * 4,
            pltpu.VMEM((devices, 1, width), jnp.float32),
            pltpu.VMEM((devices, 1, width), jnp.float32),
            pltpu.SMEM((devices, 1, width), jnp.float32),
            pltpu.VMEM((HALVES, span, half, width), jnp.float32),
            *[pltpu.VMEM((span // 2, half, width), jnp.int32)] * 4,
            pltpu.SMEM((blks, 1, width), jnp.float32),
            pltpu.VMEM((blks, 1, width), jnp.float32),
            pltpu.VMEM((blks, 1, width), jnp.float32),
            pltpu.SMEM((blks, 1, width), jnp.float32),
            pltpu.SMEM((span,), jnp.float32),
            dma((blks,)),
            dma((blks,)),
            dma((blks,)),
            dma((blks,)),
            dma((blks,)),
            dma((blks, pairs)),
            dma((blks, pairs)),
            dma((HALVES + 1, blks, pairs)),
            dma((HALVES + 1, blks, pairs)),
            dma((HALVES + 1, blks)),
            dma((HALVES + 1, blks)),
            dma((6,)),
        ],
        compiler_params=pltpu.CompilerParams(
            collective_id=0, has_side_effects=True, vmem_limit_bytes=56 * 2**20
        ),
    )(
        slab_blocks,
        *tables,
        amplitudes,
        integrals.reshape(slots, inner, width),
    )


def solution(mesh):
    placed = (P("pair", "blk"), P(("blk", "pair"), None, None, None), P(), P(), P(), P(), P())
    return jax.shard_map(
        local, mesh=mesh, in_specs=placed, out_specs=P("pair", "blk"), check_vma=False
    )
```

```python
import functools

import jax
import jax.numpy as jnp
from jax import lax
from jax.experimental import pallas as pl
from jax.experimental.pallas import tpu as pltpu
from jax.sharding import PartitionSpec as P

TOP = 32766.0
TINY = 2.0**-110
MESH = pl.DeviceIdType.MESH
HALVES = 2


def unroll_of(trips, most):
    return max(n for n in range(1, most + 1) if trips % n == 0)


def fill_tables(sizes, owner_ref, partner_ref, irrep_ref, sign_ref, irrep_out, meta_out):
    blks, pairs, span, cap, per_irrep, slab_count, rows, width = sizes
    me_blk = lax.axis_index("blk")
    me = me_blk * pairs + lax.axis_index("pair")

    down = lax.broadcasted_iota(jnp.int32, (span, span), 0)
    across = lax.broadcasted_iota(jnp.int32, (span, span), 1)
    diagonal = down == across
    earlier = down < across

    def column(row):
        return jnp.sum(jnp.where(diagonal, row, 0.0), axis=1, keepdims=True)

    def count(mask):
        return jnp.sum(jnp.where(mask, 1.0, 0.0), axis=0, keepdims=True)

    def placed(keys, values):
        hit = keys == across.astype(jnp.float32)
        return jnp.sum(jnp.where(hit, values, 0.0), axis=0, keepdims=True)

    parts = span // width

    def mine(ref):
        found = [ref[pl.ds(me_blk * parts + part, 1), :] for part in range(parts)]
        return jnp.concatenate(found, axis=1).astype(jnp.float32)

    def every(ref):
        found = [
            jnp.concatenate([ref[b * parts + part : b * parts + part + 1, :] for b in range(blks)])
            for part in range(parts)
        ]
        return jnp.concatenate(found, axis=1)

    owner, partner, sign = mine(owner_ref), mine(partner_ref), mine(sign_ref)
    partner_blk = jnp.floor((partner + 0.5) * (1.0 / span))
    owner_col, partner_col, blk_col = column(owner), column(partner), column(partner_blk)
    same_blk = blk_col == partner_blk
    rank = count(jnp.logical_and(owner_col == owner, earlier))
    send_key = partner_blk * (span // blks) + count(jnp.logical_and(same_blk, earlier))
    mirror_rank = count(jnp.logical_and(same_blk, partner_col < partner))
    key_col = column(send_key)
    send_dev = placed(key_col, owner_col)
    send_rank = placed(key_col, column(rank))
    capw, glenw = -(-cap // 2), span // blks // 2
    table = []
    for index, most, count_of, place in (
        (owner, blks * pairs, capw, rank),
        (send_dev, blks * pairs, capw, send_rank),
        (partner_blk, blks, glenw, mirror_rank),
    ):
        index = jnp.clip(index, 0.0, most - 1.0)
        place = jnp.clip(place, 0.0, min(2 * count_of, width) - 1.0)
        word = jnp.floor(place * 0.5)
        shift = 16.0 - 16.0 * (place - 2.0 * word)
        table += [index, place, index * count_of + word, shift]
    for at, row in enumerate(table + [sign]):
        meta_out[at : at + 1, :] = row.astype(jnp.int32)

    stored = every(owner_ref) == me
    ranks = jnp.dot(
        jnp.where(stored, 1.0, 0.0).astype(jnp.bfloat16),
        jnp.where(earlier, 1.0, 0.0).astype(jnp.bfloat16),
        preferred_element_type=jnp.float32,
    ).astype(jnp.int32)
    ranks = jnp.where(stored, ranks, -1)
    irrep = every(irrep_ref).astype(jnp.float32)
    lane = lax.broadcasted_iota(jnp.int32, (blks, width), 1)
    slots = jnp.zeros((blks, width), jnp.float32)
    for r in range(cap):
        found = jnp.sum(jnp.where(ranks == r, irrep, 0.0), axis=1, keepdims=True)
        slots = jnp.where(lane == r, found, slots)
    irrep_out[...] = slots.astype(jnp.int32)


def kernel(
    sizes,
    slab_hbm,
    owner_hbm,
    partner_hbm,
    irreps_hbm,
    sign_hbm,
    amp_hbm,
    ints_hbm,
    out_ref,
    slab_ref,
    owner_ref,
    partner_ref,
    irreps_ref,
    sign_ref,
    amp,
    amp_blocks,
    picked,
    irrep_v,
    meta_v,
    irrep_ref,
    meta_ref,
    ints,
    picked_in,
    slab_in,
    slab,
    send1a,
    send1b,
    recv1a,
    recv1b,
    scale1,
    scale1_in,
    scale1_s,
    own,
    send2a,
    send2b,
    recv2a,
    recv2b,
    scale2_s,
    scale2,
    scale2_in,
    scale2_in_s,
    factor_s,
    ints_sem,
    pick_send,
    pick_recv,
    gath_send,
    gath_recv,
    fwd_send,
    fwd_recv,
    send1_sem,
    recv1_sem,
    send2_sem,
    recv2_sem,
    table_sem,
    out_a,
    out_b,
    out_sem,
):
    blks, pairs, span, cap, per_irrep, slab_count, rows, width = sizes
    devices = blks * pairs
    chunk = slab_count // blks
    glen = span // blks
    me_blk = lax.axis_index("blk")
    me_pair = lax.axis_index("pair")
    me = me_blk * pairs + me_pair
    capw, glenw, half = -(-cap // 2), glen // 2, rows // 2
    lane = lax.broadcasted_iota(jnp.int32, (1, width), 1)
    send1, recv1 = (send1a, send1b), (recv1a, recv1b)
    send2, recv2 = (send2a, send2b), (recv2a, recv2b)
    out_v = (out_a, out_b)

    def blk_at(step):
        pattern = blks // 2 + (1 - step % 2) * (step // 2) - (step % 2) * ((step + 1) // 2)
        found, bit = 0, 1
        while bit < blks:
            found = found + lax.rem(me_blk // bit + pattern // bit, 2) * bit
            bit *= 2
        return found

    def ints_copy(step):
        at = blk_at(step)
        return pltpu.make_async_copy(
            ints_hbm.at[pl.ds(at * cap, cap)], ints.at[pl.ds(at * cap, cap)], ints_sem.at[step]
        )

    def table_copy(source, target, at):
        return pltpu.make_async_copy(source, target, table_sem.at[at])

    entry_copies = [
        table_copy(source, target, 6 + at)
        for at, (source, target) in enumerate(
            (
                (slab_hbm, slab_ref),
                (owner_hbm, owner_ref),
                (partner_hbm, partner_ref),
                (irreps_hbm, irreps_ref),
                (sign_hbm, sign_ref),
            )
        )
    ]
    table_copy(amp_hbm, amp, 0).start()
    for copy in entry_copies:
        copy.start()

    barrier = pltpu.get_barrier_semaphore()

    @pl.loop(0, blks - 1)
    def _(step):
        pl.semaphore_signal(barrier, inc=1, device_id={"blk": blk_at(step)}, device_id_type=MESH)

    for turn in range(1, pairs):
        pl.semaphore_signal(
            barrier, inc=1, device_id={"pair": lax.rem(me_pair + turn, pairs)}, device_id_type=MESH
        )

    @pl.loop(0, blks)
    def _(step):
        ints_copy(step).start()

    table_copy(amp_hbm, amp, 0).wait()

    def split(i, carry):
        amp_blocks[i] = amp[:, pl.ds(pl.multiple_of(i * width, width), width)]
        return carry

    lax.fori_loop(0, span, split, 0, unroll=unroll_of(span, 8))
    entry_copies[0].wait()
    for n in range(slab_count):
        local = slab_ref[n] - me_blk * span
        inside = jnp.logical_and(local >= 0, local < span).astype(jnp.float32)
        block = amp_blocks[jnp.clip(local, 0, span - 1)]
        picked[n] = (block.astype(jnp.float32) * inside).astype(jnp.bfloat16)

    pl.semaphore_wait(barrier, blks + pairs - 2)

    def pick_copy(step):
        to = blk_at(step)
        return pltpu.make_async_remote_copy(
            src_ref=picked.at[pl.ds(to * chunk, chunk)],
            dst_ref=picked_in.at[me_blk],
            send_sem=pick_send.at[step],
            recv_sem=pick_recv.at[step],
            device_id={"blk": to},
            device_id_type=MESH,
        )

    @pl.loop(0, blks - 1)
    def _(step):
        pick_copy(step).start()

    for copy in entry_copies[1:]:
        copy.wait()
    fill_tables(sizes, owner_ref, partner_ref, irreps_ref, sign_ref, irrep_v, meta_v)
    table_copy(irrep_v, irrep_ref, 1).start()
    table_copy(meta_v, meta_ref, 2).start()

    @pl.loop(0, blks - 1)
    def _(step):
        pick_copy(step).wait()

    total = picked[pl.ds(me_blk * chunk, chunk)].astype(jnp.float32)
    for step in range(blks - 1):
        total = total + picked_in[blk_at(step)].astype(jnp.float32)
    slab_in[me_pair, me_blk] = total.astype(jnp.bfloat16)

    def gath_copy(step):
        return pltpu.make_async_remote_copy(
            src_ref=slab_in.at[me_pair, me_blk],
            dst_ref=slab_in.at[me_pair, me_blk],
            send_sem=gath_send.at[step],
            recv_sem=gath_recv.at[step],
            device_id={"blk": blk_at(step)},
            device_id_type=MESH,
        )

    def fwd_copy(source_blk, step, turn):
        return pltpu.make_async_remote_copy(
            src_ref=slab_in.at[me_pair, source_blk],
            dst_ref=slab_in.at[me_pair, source_blk],
            send_sem=fwd_send.at[step, turn],
            recv_sem=fwd_recv.at[step, turn],
            device_id={"pair": lax.rem(me_pair + 1 + turn, pairs)},
            device_id_type=MESH,
        )

    @pl.loop(0, blks - 1)
    def _(step):
        gath_copy(step).start()

    for turn in range(pairs - 1):
        fwd_copy(me_blk, blks - 1, turn).start()


    @pl.loop(0, blks - 1)
    def _(step):
        gath_copy(step).wait_recv()
        for turn in range(pairs - 1):
            fwd_copy(blk_at(step), step, turn).start()

    table_copy(irrep_v, irrep_ref, 1).wait()
    table_copy(meta_v, meta_ref, 2).wait()

    def pair_at(turn):
        return lax.rem(me_pair + turn, pairs)

    def fill_slab(turns):
        for n in range(slab_count):
            columns = slice((n % per_irrep) * width, (n % per_irrep + 1) * width)
            for turn in turns:
                place = slice(turn * rows, (turn + 1) * rows)
                slab[n // per_irrep, place, columns] = slab_in[pair_at(turn), n // chunk, n % chunk]

    def products(to, turns):
        low, high = turns[0] * rows, (turns[-1] + 1) * rows

        def slots(j, scales):
            coded = []
            for turn in range(2):
                r = jnp.minimum(2 * j + turn, cap - 1)
                product = jnp.dot(
                    slab[jnp.clip(irrep_ref[to, r], 0, slab_count // per_irrep - 1), low:high],
                    ints[to * cap + r],
                    preferred_element_type=jnp.float32,
                )
                tiles, found = [], []
                for p in range(len(turns)):
                    tile = product[p * rows : (p + 1) * rows]
                    largest = jnp.max(jnp.abs(tile), axis=0, keepdims=True)
                    largest = jnp.maximum(jnp.max(largest, axis=1, keepdims=True), TINY)
                    tiles.append(jnp.round(tile * (TOP / largest)).astype(jnp.int32))
                    found.append(jnp.where(lane == r, largest * (1.0 / TOP), scales[p]))
                scales = tuple(found)
                coded.append(tiles)
            for p in range(len(turns)):
                word = (coded[0][p] & 0xFFFF) | (coded[1][p] << 16)
                for h in range(HALVES):
                    send1[h][(to * pairs + pair_at(turns[p])) * capw + j] = word[h * half : (h + 1) * half]
            return scales

        start = tuple(jnp.zeros((1, width), jnp.float32) for _ in turns)
        scales = lax.fori_loop(0, capw, slots, start, unroll=unroll_of(capw, 5))
        for p in range(len(turns)):
            scale1[to * pairs + pair_at(turns[p])] = scales[p]

    def product_copy(h, step, turn):
        to = blk_at(step)
        to_pair = lax.rem(me_pair + turn, pairs)
        at = to * pairs + to_pair
        if h == HALVES:
            source, target = scale1.at[at], scale1_in.at[me]
        else:
            source = send1[h].at[pl.ds(at * capw, capw)]
            target = recv1[h].at[pl.ds(me * capw, capw)]
        return pltpu.make_async_remote_copy(
            src_ref=source,
            dst_ref=target,
            send_sem=send1_sem.at[h, step, turn],
            recv_sem=recv1_sem.at[h, step, turn],
            device_id={"blk": to, "pair": to_pair},
            device_id_type=MESH,
        )

    def keep_copy(h):
        if h == HALVES:
            source, target = scale1.at[me], scale1_in.at[me]
        else:
            source = send1[h].at[pl.ds(me * capw, capw)]
            target = recv1[h].at[pl.ds(me * capw, capw)]
        return pltpu.make_async_copy(source, target, send1_sem.at[h, blks - 1, 0])

    def send_products(h):
        for turn in range(1, pairs):
            product_copy(h, 0, turn).start()

        @pl.loop(1, blks - 1)
        def _(step):
            for turn in range(pairs):
                product_copy(h, step, turn).start()

        keep_copy(h).start()
        for turn in range(1, pairs):
            product_copy(h, blks - 1, turn).start()

    def wait_products(h):
        keep_copy(h).wait()

        @pl.loop(0, blks - 1)
        def _(step):
            for turn in range(pairs):
                product_copy(h, step, turn).wait()

        for turn in range(1, pairs):
            product_copy(h, blks - 1, turn).wait()

    ints_copy(0).wait()
    fill_slab([0])
    products(blk_at(0), [0])
    for h in (HALVES, 0, 1):
        product_copy(h, 0, 0).start()

    @pl.loop(0, blks - 1)
    def _(step):
        gath_copy(step).wait_send()

    @pl.loop(0, blks)
    def _(step):
        for turn in range(pairs - 1):
            fwd_copy(blk_at(step), step, turn).wait()

    every_turn = list(range(pairs))
    fill_slab(every_turn[1:])
    products(blk_at(0), every_turn[1:])
    for h in (HALVES, 0):
        for turn in range(1, pairs):
            product_copy(h, 0, turn).start()

    @pl.loop(1, blks - 1)
    def _(step):
        ints_copy(step).wait()
        products(blk_at(step), every_turn)
        for h in (HALVES, 0):
            for turn in range(pairs):
                product_copy(h, step, turn).start()

    ints_copy(blks - 1).wait()
    products(me_blk, every_turn)
    for h in (HALVES, 0):
        keep_copy(h).start()
        for turn in range(1, pairs):
            product_copy(h, blks - 1, turn).start()
    send_products(1)

    def mirror_copy(h, step):
        to = blk_at(step)
        if h == HALVES:
            source, target = scale2.at[to], scale2_in.at[me_blk]
        else:
            source = send2[h].at[pl.ds(to * glenw, glenw)]
            target = recv2[h].at[pl.ds(me_blk * glenw, glenw)]
        return pltpu.make_async_remote_copy(
            src_ref=source,
            dst_ref=target,
            send_sem=send2_sem.at[h, step],
            recv_sem=recv2_sem.at[h, step],
            device_id={"blk": to, "pair": lax.rem(me_pair + pairs // 2, pairs)},
            device_id_type=MESH,
        )

    def value_of(word, shift):
        return ((word << shift) >> 16).astype(jnp.float32)

    def gather(h):
        @pl.loop(0, blks)
        def _(step):
            to = blk_at(step)

            def entry(m, carry):
                i = to * glen + 2 * m
                low = recv1[h][jnp.clip(meta_ref[6, i], 0, devices * capw - 1)] << meta_ref[7, i]
                high = recv1[h][jnp.clip(meta_ref[6, i + 1], 0, devices * capw - 1)] << meta_ref[7, i + 1]
                send2[h][to * glenw + m] = lax.shift_right_logical(low, 16) | (high & -65536)
                return carry

            lax.fori_loop(0, glenw, entry, 0, unroll=unroll_of(glenw, 8))
            mirror_copy(h, step).start()

        def own_entry(i, carry):
            scale = scale1_s[jnp.clip(meta_ref[0, i], 0, devices - 1), 0, jnp.clip(meta_ref[1, i], 0, width - 1)]
            own[h, i] = value_of(recv1[h][jnp.clip(meta_ref[2, i], 0, devices * capw - 1)], meta_ref[3, i]) * scale
            return carry

        lax.fori_loop(0, span, own_entry, 0, unroll=unroll_of(span, 8))

    def finish(h):
        def out_entry(i, carry):
            if h == 0:
                place = (jnp.clip(meta_ref[8, i], 0, blks - 1), jnp.clip(meta_ref[9, i], 0, width - 1))
                scale = scale2_in_s[place[0], 0, place[1]] * meta_ref[12, i].astype(jnp.float32)
                factor_s[i] = scale
            else:
                scale = factor_s[i]
            mirrored = value_of(recv2[h][jnp.clip(meta_ref[10, i], 0, span // 2 - 1)], meta_ref[11, i])
            total = own[h, i] + mirrored * scale
            columns = pl.ds(pl.multiple_of(i * width, width), width)
            out_v[h][:, columns] = total.astype(jnp.bfloat16)
            return carry

        copies = []
        for part in range(4):
            low, high = part * span // 4, (part + 1) * span // 4
            lax.fori_loop(low, high, out_entry, 0, unroll=unroll_of(high - low, 8))
            columns = slice(low * width, high * width)
            copy = pltpu.make_async_copy(
                out_v[h].at[:, columns],
                out_ref.at[h * half : (h + 1) * half, columns],
                out_sem.at[h, part],
            )
            copy.start()
            copies.append(copy)
        return copies

    wait_products(HALVES)
    table_copy(scale1_in, scale1_s, 3).start()
    table_copy(scale1_in, scale1_s, 3).wait()

    def scale_entry(i, carry):
        scale2_s[i // glen, 0, i % glen] = scale1_s[jnp.clip(meta_ref[4, i], 0, devices - 1), 0, jnp.clip(meta_ref[5, i], 0, width - 1)]
        return carry

    lax.fori_loop(0, span, scale_entry, 0, unroll=unroll_of(span, 8))
    table_copy(scale2_s, scale2, 4).start()
    table_copy(scale2_s, scale2, 4).wait()

    @pl.loop(0, blks)
    def _(step):
        mirror_copy(HALVES, step).start()

    wait_products(0)
    gather(0)

    @pl.loop(0, blks)
    def _(step):
        mirror_copy(HALVES, step).wait()

    table_copy(scale2_in, scale2_in_s, 5).start()
    table_copy(scale2_in, scale2_in_s, 5).wait()
    wait_products(1)
    gather(1)
    outs = []
    for h in range(HALVES):

        @pl.loop(0, blks)
        def _(step):
            mirror_copy(h, step).wait()

        outs += finish(h)
    for copy in outs:
        copy.wait()


def local(amplitudes, integrals, block_irrep, slab_blocks, owner, partner, sign):
    rows, columns = amplitudes.shape
    slots, per_irrep, _, width = integrals.shape
    blks = lax.axis_size("blk")
    pairs = lax.axis_size("pair")
    devices = blks * pairs
    span = columns // width
    cap = slots // blks
    glen = span // blks
    slab_count = slab_blocks.shape[0]
    irreps = slab_count // per_irrep
    chunk = slab_count // blks
    inner = per_irrep * width
    capw, half = -(-cap // 2), rows // 2
    tables = [table.reshape(-1, width) for table in (owner, partner, block_irrep, sign)]

    sizes = (blks, pairs, span, cap, per_irrep, slab_count, rows, width)
    dma = pltpu.SemaphoreType.DMA
    hbm = pl.BlockSpec(memory_space=pl.ANY)
    return pl.pallas_call(
        functools.partial(kernel, sizes),
        out_shape=jax.ShapeDtypeStruct((rows, columns), jnp.bfloat16),
        in_specs=[hbm] * 7,
        out_specs=hbm,
        scratch_shapes=[
            pltpu.SMEM(slab_blocks.shape, jnp.int32),
            *[pltpu.VMEM(table.shape, jnp.int32) for table in tables],
            pltpu.VMEM((rows, columns), jnp.bfloat16),
            pltpu.VMEM((span, rows, width), jnp.bfloat16),
            pltpu.VMEM((slab_count, rows, width), jnp.bfloat16),
            pltpu.VMEM((blks, width), jnp.int32),
            pltpu.VMEM((16, span), jnp.int32),
            pltpu.SMEM((blks, width), jnp.int32),
            pltpu.SMEM((16, span), jnp.int32),
            pltpu.VMEM((slots, inner, width), jnp.bfloat16),
            pltpu.VMEM((blks, chunk, rows, width), jnp.bfloat16),
            pltpu.VMEM((pairs, blks, chunk, rows, width), jnp.bfloat16),
            pltpu.VMEM((irreps, rows * pairs, inner), jnp.bfloat16),
            *[pltpu.VMEM((devices * capw, half, width), jnp.int32)] * 4,
            pltpu.VMEM((devices, 1, width), jnp.float32),
            pltpu.VMEM((devices, 1, width), jnp.float32),
            pltpu.SMEM((devices, 1, width), jnp.float32),
            pltpu.VMEM((HALVES, span, half, width), jnp.float32),
            *[pltpu.VMEM((span // 2, half, width), jnp.int32)] * 4,
            pltpu.SMEM((blks, 1, width), jnp.float32),
            pltpu.VMEM((blks, 1, width), jnp.float32),
            pltpu.VMEM((blks, 1, width), jnp.float32),
            pltpu.SMEM((blks, 1, width), jnp.float32),
            pltpu.SMEM((span,), jnp.float32),
            dma((blks,)),
            dma((blks,)),
            dma((blks,)),
            dma((blks,)),
            dma((blks,)),
            dma((blks, pairs)),
            dma((blks, pairs)),
            dma((HALVES + 1, blks, pairs)),
            dma((HALVES + 1, blks, pairs)),
            dma((HALVES + 1, blks)),
            dma((HALVES + 1, blks)),
            dma((11,)),
            *[pltpu.VMEM((half, columns), jnp.bfloat16)] * HALVES,
            dma((HALVES, 4)),
        ],
        compiler_params=pltpu.CompilerParams(
            collective_id=0, has_side_effects=True, vmem_limit_bytes=56 * 2**20
        ),
    )(
        slab_blocks,
        *tables,
        amplitudes,
        integrals.reshape(slots, inner, width),
    )


def solution(mesh):
    placed = (P("pair", "blk"), P(("blk", "pair"), None, None, None), P(), P(), P(), P(), P())
    return jax.shard_map(
        local, mesh=mesh, in_specs=placed, out_specs=P("pair", "blk"), check_vma=False
    )
```
